256 devices in a mesh: space: 32 (over y, z), tm: 8 (over x, core).
Axes of the slice: x: 4, y: 4, z: 8, core: 2. Of those that a mesh axis runs over, the one named last changes fastest.
Arguments:
- snapshots: float32 [4096, 98304], P('tm', 'space')
- sample_phase: int32 [4, 8], replicated, may hold values from 0 to 15, as said below
Outputs:
- residual: float32 [4096, 98304], P('tm', 'space')
The draws below stay inside these ranges and needn't reach their ends.
Inputs may be any that keep to these rules, and one draw needn't show every extreme that they name: sample_phase[l, w] lies below 4096 / (256 2^l); entries with w >= 2^l are never read.
All inputs are finite; a program needn't handle non-finite values.
Results may differ from the reference program's by a relative error of at most 0.0001.
Values sent between devices are 32-bit elements; how exact they have to be, the bound alone decides.
A program may use at most 64 MiB of HBM per device.

```python
import math
import jax
import jax.numpy as jnp
from jax import lax

POINTS = 98304
SNAPS = 4096
NSUB = 256
RANK = 32
LEVELS = 4
WMAX = 8


def draw_snapshots(key, part):
    keys_all = jax.random.split(key, 3)
    base_draw = jax.random.normal(keys_all[0], (SNAPS, POINTS), jnp.float32)
    point_scale = jnp.exp(jax.random.uniform(keys_all[1], (1, POINTS), jnp.float32, 0.0, 0.5 * math.log(10.0)))
    time_scale = jnp.exp(jax.random.uniform(keys_all[2], (SNAPS, 1), jnp.float32, 0.0, 0.5 * math.log(10.0)))
    values = base_draw * point_scale * time_scale / 3.0
    return values


def draw_sample_phase(key, part):
    tiers = jnp.arange(LEVELS, dtype=jnp.int32)
    strides = SNAPS // NSUB // 2 ** tiers
    drawn = jax.random.randint(key, (LEVELS, WMAX), 0, strides[:, None], dtype=jnp.int32)
    drawn = drawn.at[0, WMAX - 1].set(SNAPS // NSUB - 1)
    drawn = drawn.at[0, WMAX - 2].set(0)
    return drawn


def setup_inputs(seed: int = 0) -> dict:
    key_of = jax.random.split(jax.random.key(seed), 3)
    return {
        "snapshots": draw_snapshots(jax.random.fold_in(key_of[2], 71), 0),
        "sample_phase": draw_sample_phase(jax.random.fold_in(key_of[2], 71), 0),
    }


precise = lax.Precision.HIGHEST

def cosine_table(position):
    frequency = jnp.arange(RANK, dtype=jnp.float32)
    weights = jnp.where(frequency == 0.0, math.sqrt(1.0 / NSUB), math.sqrt(2.0 / NSUB)).astype(jnp.float32)
    return jnp.cos(math.pi * (position[:, None] + 0.5) * frequency[None, :] / NSUB) * weights[None, :]

def amplitudes(reduced, window_phase, stride, first_row, count_rows):
    sampled_basis = cosine_table(jnp.arange(NSUB, dtype=jnp.float32))
    earlier = reduced[:, :-1]
    following = reduced[:, 1:]
    identity = jnp.eye(RANK, dtype=jnp.float32)
    lag_gram = jnp.dot(earlier, earlier.T, precision=precise)
    cross_gram = jnp.dot(following, earlier.T, precision=precise)
    ridge_one = 0.1 * jnp.trace(lag_gram) / RANK
    factor_one = jnp.linalg.cholesky(lag_gram + ridge_one * identity)
    operator = jax.scipy.linalg.cho_solve((factor_one, True), cross_gram.T).T
    predicted = jnp.concatenate([reduced[:, :1], jnp.dot(operator, earlier, precision=precise)], axis=1)
    smooth_coef = jnp.dot(predicted, sampled_basis, precision=precise)
    mode_gram = jnp.dot(reduced, sampled_basis, precision=precise)
    mode_gram = 0.5 * (mode_gram + mode_gram.T)
    ridge_two = 0.1 * jnp.trace(mode_gram) / RANK
    factor_two = jnp.linalg.cholesky(mode_gram + ridge_two * identity)
    coefficients = jax.scipy.linalg.cho_solve((factor_two, True), smooth_coef)
    rows_index = first_row + jnp.arange(count_rows, dtype=jnp.int32)
    position = (rows_index - window_phase).astype(jnp.float32) / stride
    return jnp.dot(coefficients, cosine_table(position).T, precision=precise)

def reference(snapshots, sample_phase):
    residual = snapshots
    sampled_basis = cosine_table(jnp.arange(NSUB, dtype=jnp.float32))
    for tier_index in range(LEVELS):
        width_rows = SNAPS // 2 ** tier_index
        stride = width_rows // NSUB
        pieces = []
        for window in range(2 ** tier_index):
            block_rows = residual[window * width_rows:(window + 1) * width_rows]
            window_phase = sample_phase[tier_index, window]
            sampled = lax.dynamic_index_in_dim(block_rows.reshape(NSUB, stride, POINTS), window_phase, axis=1, keepdims=False)
            coords = jnp.dot(sampled_basis.T, sampled, precision=precise)
            reduced = jnp.dot(coords, sampled.T, precision=precise)
            amplitude = amplitudes(reduced, window_phase, stride, 0, width_rows)
            fitted = jnp.dot(amplitude.T, coords, precision=precise)
            pieces.append(block_rows - fitted)
        residual = jnp.concatenate(pieces, axis=0)
    return residual
```

```python
import functools
import math

import jax
import jax.numpy as jnp
import numpy as np
from jax import lax
from jax.experimental import pallas as pl
from jax.experimental.pallas import tpu as pltpu
from jax.sharding import PartitionSpec as P

NSUB = 256
RANK = 32
LEVELS = 4
PATH = RANK * LEVELS
ROWS = 512
COLS = 3072
HALF = COLS // 2
PIECE = HALF // 4
CHUNKS = 32
PACKET = 24
MESH = pl.DeviceIdType.MESH
f32 = jnp.float32
bf16 = jnp.bfloat16
VLIM = 60 * 1024 * 1024


def make_constants():
    j = np.arange(RANK)
    cj = np.where(j == 0, math.sqrt(1.0 / NSUB), math.sqrt(2.0 / NSUB))
    r = np.arange(ROWS)[:, None]
    cos_rows, sin_rows = [], []
    for m in range(LEVELS):
        s = 16 >> m
        ang = math.pi * j * (r + s / 2.0) / (256.0 * s)
        cos_rows.append(cj * np.cos(ang))
        sin_rows.append(cj * np.sin(ang))
    cos_rows = np.concatenate(cos_rows, 1).astype(np.float32)
    sin_rows = np.concatenate(sin_rows, 1).astype(np.float32)
    k = np.arange(NSUB)[:, None]
    bc = np.zeros((3, NSUB, PATH))
    bs = np.zeros((3, NSUB, PATH))
    for l in range(1, LEVELS):
        for m in range(l):
            ang = math.pi * j * (k * 2.0 ** (m - l) + 0.5) / 256.0
            bc[l - 1, :, m * RANK : (m + 1) * RANK] = cj * np.cos(ang)
            bs[l - 1, :, m * RANK : (m + 1) * RANK] = cj * np.sin(ang)
    q = cj * np.cos(math.pi * j * (k + 0.5) / 256.0)
    qpad = np.zeros((NSUB, PATH))
    qpad[:, :RANK] = q
    wq = np.zeros((NSUB, PATH))
    wq[: NSUB - 1, 64:96] = q[1:]
    wq[:, 96:128] = q
    first = np.zeros((NSUB, PATH))
    first[0, 64:96] = q[0]
    small = np.stack([qpad, wq, first]).astype(np.float32)
    return cos_rows, sin_rows, bc.astype(np.float32), bs.astype(np.float32), small


def cos_sin(num, period):
    frac = num.astype(f32) * (1.0 / period.astype(f32))
    quarter = jnp.floor(frac * 4.0 + 0.5)
    a = (frac - quarter * 0.25) * (2.0 * math.pi)
    a2 = a * a
    c = 1.0 + a2 * (-0.5 + a2 * (1 / 24.0 + a2 * (-1 / 720.0 + a2 * (1 / 40320.0))))
    s = a * (1.0 + a2 * (-1 / 6.0 + a2 * (1 / 120.0 + a2 * (-1 / 5040.0 + a2 * (1 / 362880.0)))))
    qi = quarter.astype(jnp.int32) & 3
    cosv = jnp.where(qi == 0, c, jnp.where(qi == 1, -s, jnp.where(qi == 2, -c, s)))
    sinv = jnp.where(qi == 0, s, jnp.where(qi == 1, c, jnp.where(qi == 2, -s, -c)))
    return cosv, sinv


def path_phases(phase_ref, t):
    return [phase_ref[m, t // (8 >> m)] for m in range(LEVELS)]


def pick(level, values):
    out = jnp.where(level == 0, values[0], values[1])
    out = jnp.where(level == 2, values[2], out)
    return jnp.where(level == 3, values[3], out)


def lane_turn(idx, offsets):
    level, j = idx // RANK, idx % RANK
    period = pick(level, [512 * 16, 512 * 8, 512 * 4, 512 * 2])
    num = (j * pick(level, offsets)) & (period - 1)
    return cos_sin(num, period)


def split(x):
    hi = x.astype(bf16)
    lo = (x - hi.astype(f32)).astype(bf16)
    return hi, lo


def dot(a, b, dims):
    return lax.dot_general(a, b, (dims, ((), ())), preferred_element_type=f32)


def dot32(a, b, ca, cb):
    return lax.dot_general(
        a, b, (((ca,), (cb,)), ((), ())), precision=lax.Precision.HIGHEST, preferred_element_type=f32
    )


def project_kernel(phase_ref, cos_ref, sin_ref, x_ref, p_ref, d_ref):
    @pl.when(pl.program_id(0) == 0)
    def _():
        t = lax.axis_index("tm")
        ps = path_phases(phase_ref, t)
        idx = lax.broadcasted_iota(jnp.int32, (PATH, 1), 0)
        offsets = [(t % (8 >> m)) * ROWS - ps[m] for m in range(LEVELS)]
        c, s = lane_turn(idx, offsets)
        level = idx // RANK
        r = lax.broadcasted_iota(jnp.int32, (PATH, ROWS), 1)
        stride = pick(level, [16, 8, 4, 2])
        on = ((r - pick(level, ps)) & (stride - 1)) == 0
        d = jnp.where(on, cos_ref[...] * c - sin_ref[...] * s, 0.0)
        hi, lo = split(d)
        d_ref[:PATH, :] = hi
        d_ref[PATH:, :] = lo

    xh, xl = split(x_ref[...])
    d = d_ref[...]
    a = dot(d, xh, ((1,), (0,)))
    b = dot(d[:PATH], xl, ((1,), (0,)))
    p_ref[...] = a[:PATH] + (a[PATH:] + b)


def project(phase, cos_t, sin_t, x):
    tile = 512
    return pl.pallas_call(
        project_kernel,
        grid=(COLS // tile,),
        in_specs=[
            pl.BlockSpec(memory_space=pltpu.SMEM),
            pl.BlockSpec((PATH, ROWS), lambda i: (0, 0)),
            pl.BlockSpec((PATH, ROWS), lambda i: (0, 0)),
            pl.BlockSpec((ROWS, tile), lambda i: (0, i)),
        ],
        out_specs=pl.BlockSpec((PATH, tile), lambda i: (0, i)),
        out_shape=jax.ShapeDtypeStruct((PATH, COLS), f32),
        scratch_shapes=[pltpu.VMEM((2 * PATH, ROWS), bf16)],
        compiler_params=pltpu.CompilerParams(vmem_limit_bytes=VLIM),
        name="project",
    )(phase, cos_t, sin_t, x)


def remote(src, dst, send, recv, where):
    return pltpu.make_async_remote_copy(
        src_ref=src, dst_ref=dst, send_sem=send, recv_sem=recv, device_id=where, device_id_type=MESH
    )


def sum_kernel(p_ref, y_ref, r1, s0, s1, r2, r3, ssem, rsem):
    t = lax.axis_index("tm")
    x, h = t // 2, t % 2
    partner = {"tm": x * 2 + 1 - h}
    across = [{"tm": lax.rem(x + d, 4) * 2 + h} for d in range(1, 4)]
    pair = {"tm": (x + 1 - 2 * (x % 2)) * 2 + h}
    barrier = pltpu.get_barrier_semaphore()
    for dev in [partner] + across:
        pl.semaphore_signal(barrier, inc=1, device_id=dev, device_id_type=MESH)
    pl.semaphore_wait(barrier, 4)

    mine = pl.multiple_of(h * HALF, 128)
    other = pl.multiple_of((1 - h) * HALF, 128)
    own = pl.ds(mine, HALF)
    live = []

    def go(i, src, dst, where):
        c = remote(src, dst, ssem.at[i], rsem.at[i], where)
        c.start()
        live.append(c)
        return c

    first = [
        go(l, p_ref.at[pl.ds(32 * l, 32), pl.ds(other, HALF)], r1.at[l], partner) for l in range(3)
    ]
    y_ref[96:128, :] = p_ref[96:128, :]
    first[0].wait_recv()
    s0[...] = p_ref[0:32, own] + r1[0]
    spread = []
    for d in range(1, 4):
        col = pl.multiple_of(lax.rem(x + d, 4) * PIECE, 128)
        spread.append(go(2 + d, s0.at[:, pl.ds(col, PIECE)], r3.at[d - 1], across[d - 1]))
    first[1].wait_recv()
    s1[...] = p_ref[32:64, own] + r1[1]
    swap = go(6, s1, r2, pair)
    first[2].wait_recv()
    y_ref[64:96, own] = p_ref[64:96, own] + r1[2]
    last2 = go(7, y_ref.at[64:96, own], y_ref.at[64:96, own], partner)
    for c in spread:
        c.wait_recv()
    spot = pl.ds(pl.multiple_of(mine + x * PIECE, 128), PIECE)
    y_ref[0:32, spot] = (s0[:, pl.ds(pl.multiple_of(x * PIECE, 128), PIECE)] + r3[0]) + (r3[1] + r3[2])
    place = y_ref.at[0:32, spot]
    back = [go(8 + d, place, place, across[d - 1]) for d in range(1, 4)]
    pass_on = [go(12, place, place, partner)]
    swap.wait_recv()
    y_ref[32:64, own] = s1[...] + r2[...]
    last1 = go(13, y_ref.at[32:64, own], y_ref.at[32:64, own], partner)
    for d in range(1, 4):
        back[d - 1].wait_recv()
        got = pl.ds(pl.multiple_of(mine + lax.rem(x + 4 - d, 4) * PIECE, 128), PIECE)
        pass_on.append(go(13 + d, y_ref.at[0:32, got], y_ref.at[0:32, got], partner))
    for c in pass_on + [last1, last2]:
        c.wait_recv()
    for c in live:
        c.wait_send()


def sum_over_time(p):
    return pl.pallas_call(
        sum_kernel,
        in_specs=[pl.BlockSpec(memory_space=pltpu.VMEM)],
        out_specs=pl.BlockSpec(memory_space=pltpu.VMEM),
        out_shape=jax.ShapeDtypeStruct((PATH, COLS), f32),
        scratch_shapes=[
            pltpu.VMEM((3, RANK, HALF), f32),
            pltpu.VMEM((RANK, HALF), f32),
            pltpu.VMEM((RANK, HALF), f32),
            pltpu.VMEM((RANK, HALF), f32),
            pltpu.VMEM((3, RANK, PIECE), f32),
            pltpu.SemaphoreType.DMA((17,)),
            pltpu.SemaphoreType.DMA((17,)),
        ],
        compiler_params=pltpu.CompilerParams(
            collective_id=0, has_side_effects=True, vmem_limit_bytes=VLIM
        ),
        name="sum_over_time",
    )(p)


def product_kernel(phase_ref, x_ref, y_ref, f_ref, acc):
    i = pl.program_id(0)
    xh, xl = split(x_ref[...])
    yh, yl = split(y_ref[...])
    both = jnp.concatenate([yh, yl], axis=0)
    a = dot(xh, both, ((1,), (1,)))
    b = dot(xl, yh, ((1,), (1,)))
    new = a[:, :PATH] + (a[:, PATH:] + b)

    @pl.when(i == 0)
    def _():
        acc[...] = new

    @pl.when(i > 0)
    def _():
        acc[...] += new

    @pl.when(i == pl.num_programs(0) - 1)
    def _():
        t = lax.axis_index("tm")
        ps = path_phases(phase_ref, t)
        row = 0
        for l in (3, 2, 1, 0):
            for e in range(1 << l):
                start = ps[l] + e * (16 >> l)
                f_ref[pl.ds(row, CHUNKS, stride=16), :] = acc[pl.ds(start, CHUNKS, stride=16), :]
                row += 1
        f_ref[pl.ds(row, CHUNKS, stride=16), :] = jnp.zeros((CHUNKS, PATH), f32)


def products(phase, x, y):
    tile = 512
    return pl.pallas_call(
        product_kernel,
        grid=(COLS // tile,),
        in_specs=[
            pl.BlockSpec(memory_space=pltpu.SMEM),
            pl.BlockSpec((ROWS, tile), lambda i: (0, i)),
            pl.BlockSpec((PATH, tile), lambda i: (0, i)),
        ],
        out_specs=pl.BlockSpec((ROWS, PATH), lambda i: (0, 0)),
        out_shape=jax.ShapeDtypeStruct((ROWS, PATH), f32),
        scratch_shapes=[pltpu.VMEM((ROWS, PATH), f32)],
        compiler_params=pltpu.CompilerParams(vmem_limit_bytes=VLIM),
        name="products",
    )(phase, x, y)


def gather_kernel(f_ref, g_ref, ry, q, rz, xb, cb, ssem, rsem):
    s = lax.axis_index("space")
    t = lax.axis_index("tm")
    y, z = s // 8, s % 8
    ys = [lax.rem(y + d, 4) for d in range(1, 4)]
    zs = [lax.rem(z + d, 8) for d in range(1, 8)]
    ts = [lax.rem(t + d, 8) for d in range(1, 8)]
    to_y = [{"space": v * 8 + z} for v in ys]
    to_z = [{"space": y * 8 + v} for v in zs]
    to_t = [{"tm": v} for v in ts]
    barrier = pltpu.get_barrier_semaphore()
    for dev in to_y + to_z + to_t:
        pl.semaphore_signal(barrier, inc=1, device_id=dev, device_id_type=MESH)
    pl.semaphore_wait(barrier, 17)
    live = []

    def go(i, src, dst, where):
        c = remote(src, dst, ssem.at[i], rsem.at[i], where)
        c.start()
        live.append(c)
        return c

    def rows(start, n):
        return pl.ds(pl.multiple_of(start, 8), n)

    a = [go(d, f_ref.at[rows(ys[d] * 128, 128)], ry.at[d], to_y[d]) for d in range(3)]
    for c in a:
        c.wait_recv()
    q[...] = (f_ref[rows(y * 128, 128), :] + ry[0]) + (ry[1] + ry[2])
    a = [go(3 + d, q.at[rows(zs[d] * 16, 16)], rz.at[d], to_z[d]) for d in range(7)]
    for c in a:
        c.wait_recv()
    ch = q[rows(z * 16, 16), :] + rz[0]
    for d in range(1, 7):
        ch = ch + rz[d]
    base = s * PACKET
    g_ref[rows(base, 8), :] = ch[0:8]
    xb[t] = ch[8:16]
    a = [go(10 + d, xb.at[t], xb.at[t], to_t[d]) for d in range(7)]
    for c in a:
        c.wait_recv()
    pair = t // 2 * 2
    quad = t // 4 * 4
    g_ref[rows(base + 8, 8), :] = jnp.concatenate([xb[pair][0:4], xb[pair + 1][0:4]], axis=0)
    for i in range(4):
        cb[2 * i : 2 * i + 2, :] = xb[quad + i][4:6]
    for i in range(8):
        cb[8 + i : 9 + i, :] = xb[i][6:7]
    lane = lax.broadcasted_iota(jnp.int32, (8, PATH), 1)
    g_ref[rows(base + 16, 8), :] = jnp.where(lane < 64, cb[0:8, :], pltpu.roll(cb[8:16, :], 64, 1))
    piece = g_ref.at[rows(base, PACKET)]
    a = [go(17 + d, piece, piece, to_z[d]) for d in range(7)]
    for c in a:
        c.wait_recv()
    band = g_ref.at[rows(y * 8 * PACKET, 8 * PACKET)]
    a = [go(24 + d, band, band, to_y[d]) for d in range(3)]
    for c in a:
        c.wait_recv()
    for c in live:
        c.wait_send()


def gather(f):
    return pl.pallas_call(
        gather_kernel,
        in_specs=[pl.BlockSpec(memory_space=pltpu.VMEM)],
        out_specs=pl.BlockSpec(memory_space=pltpu.VMEM),
        out_shape=jax.ShapeDtypeStruct((CHUNKS * PACKET, PATH), f32),
        scratch_shapes=[
            pltpu.VMEM((3, 128, PATH), f32),
            pltpu.VMEM((128, PATH), f32),
            pltpu.VMEM((7, 16, PATH), f32),
            pltpu.VMEM((8, 8, PATH), f32),
            pltpu.VMEM((16, PATH), f32),
            pltpu.SemaphoreType.DMA((27,)),
            pltpu.SemaphoreType.DMA((27,)),
        ],
        compiler_params=pltpu.CompilerParams(
            collective_id=1, has_side_effects=True, vmem_limit_bytes=VLIM
        ),
        name="gather",
    )(f)


def eliminate(a, b):
    sub = lax.broadcasted_iota(jnp.int32, (RANK, 1), 0)
    for k in range(RANK):
        ra = a[k : k + 1, :]
        rb = b[k : k + 1, :]
        ra = ra / a[k : k + 1, k : k + 1]
        rb = rb / b[k : k + 1, k : k + 1]
        a = jnp.where(sub == k, ra, a - a[:, k : k + 1] * ra)
        b = jnp.where(sub == k, rb, b - b[:, k : k + 1] * rb)
    return a, b


def solve_kernel(phase_ref, bc_ref, bs_ref, small_ref, g_ref, n_ref, lv):
    t = lax.axis_index("tm")
    ps = path_phases(phase_ref, t)
    lane = lax.broadcasted_iota(jnp.int32, (1, PATH), 1)
    row = lax.broadcasted_iota(jnp.int32, (NSUB, 1), 0)
    big = CHUNKS * PACKET
    for c in range(CHUNKS):
        lv[3, 8 * c : 8 * c + 8, :] = g_ref[PACKET * c : PACKET * c + 8, :]
    for i in range(2):
        for e in range(4):
            lv[2, pl.ds(128 * i + e, CHUNKS, stride=4), :] = g_ref[
                pl.ds(8 + 4 * i + e, CHUNKS, stride=PACKET), :
            ]
    for i in range(4):
        for e in range(2):
            lv[1, pl.ds(64 * i + e, CHUNKS, stride=2), :] = g_ref[
                pl.ds(16 + 2 * i + e, CHUNKS, stride=PACKET), :
            ]
    for i in range(8):
        lv[0, 32 * i : 32 * i + 32, :] = pltpu.roll(
            g_ref[pl.ds(16 + i, CHUNKS, stride=PACKET), :], 64, 1
        )
    qpad = small_ref[0]
    wq = small_ref[1]
    first = small_ref[2]
    seen = []
    gram = []
    for l in range(LEVELS):
        m = jnp.where(lane < RANK * (l + 1), lv[l], 0.0)
        seen.append(m)
        gram.append(dot32(qpad, m, 0, 0)[:RANK])
    low = jnp.concatenate(gram, axis=0)
    up = low.T
    rb = lax.broadcasted_iota(jnp.int32, (PATH, PATH), 0) // RANK
    cb = lax.broadcasted_iota(jnp.int32, (PATH, PATH), 1) // RANK
    gram = jnp.where(cb <= rb, low, up)
    tables, folded = [None], [None]
    for l in range(1, LEVELS):
        here = (t // (8 >> l)) * (ROWS * (8 >> l)) + ps[l]
        offsets = [here - (t // (8 >> m)) * (ROWS * (8 >> m)) - ps[m] for m in range(LEVELS)]
        c, s = lane_turn(lane, offsets)
        table = bc_ref[l - 1] * c - bs_ref[l - 1] * s
        tables.append(table)
        folded.append(dot32(qpad, table, 0, 0)[:RANK])
    sub = lax.broadcasted_iota(jnp.int32, (RANK, PATH), 0)
    lan = lax.broadcasted_iota(jnp.int32, (RANK, PATH), 1)
    eye = (sub == lan).astype(f32)
    eye_next = (sub + RANK == lan).astype(f32)
    n = jnp.zeros((PATH, PATH), f32)
    nk = jnp.zeros((PATH, PATH), f32)
    for l in range(LEVELS):
        comb = (sub + RANK * l == lan).astype(f32)
        part = seen[l]
        if l:
            comb = comb - dot32(folded[l], n, 1, 0)
            part = part - dot32(tables[l], nk, 1, 0)
        wide = jnp.concatenate([comb, jnp.zeros((PATH - RANK, PATH), f32)], axis=0)
        rt = dot32(part, wide, 1, 1)
        right = (
            jnp.where(row < NSUB - 1, rt, 0.0)
            + pltpu.roll(jnp.where(row > 0, pltpu.roll(rt, RANK, 1), 0.0), NSUB - 1, 0)
            + wq
        )
        narrow = rt[:, :RANK]
        w = dot32(narrow, right, 0, 0)
        head = dot32(narrow, first, 0, 0)
        wt = dot32(qpad[:, :RANK], rt, 0, 0)
        ridge_one = 0.1 / RANK * jnp.sum(w * eye)
        mode = jnp.where(lan < RANK, 0.5 * (pltpu.roll(w, RANK, 1) + wt), 0.0)
        ridge_two = 0.1 / RANK * jnp.sum(mode * eye)
        a, b = eliminate(w + ridge_one * eye, mode + ridge_two * eye + eye_next)
        smooth = head + dot32(w, a, 0, 0)[RANK : 2 * RANK]
        coef = dot32(b, smooth, 0, 0)[RANK : 2 * RANK]
        new = dot32(coef, comb, 0, 0)[64:96]
        n_ref[RANK * l : RANK * (l + 1), :] = new
        if l < LEVELS - 1:
            before = [n[: RANK * l]] if l else []
            after = [jnp.zeros((PATH - RANK * (l + 1), PATH), f32)]
            n = jnp.concatenate(before + [new] + after, axis=0)
            before = [nk[: RANK * l]] if l else []
            nk = jnp.concatenate(before + [dot32(new, gram, 1, 0)] + after, axis=0)


def solve(phase, bc, bs, small, g):
    vm = pl.BlockSpec(memory_space=pltpu.VMEM)
    return pl.pallas_call(
        solve_kernel,
        in_specs=[pl.BlockSpec(memory_space=pltpu.SMEM), vm, vm, vm, vm],
        out_specs=vm,
        out_shape=jax.ShapeDtypeStruct((PATH, PATH), f32),
        scratch_shapes=[pltpu.VMEM((LEVELS, NSUB, PATH), f32)],
        compiler_params=pltpu.CompilerParams(vmem_limit_bytes=VLIM),
        name="solve",
    )(phase, bc, bs, small, g)


def subtract_kernel(phase_ref, cos_ref, sin_ref, n_ref, x_ref, y_ref, o_ref, e_ref):
    @pl.when(pl.program_id(0) == 0)
    def _():
        t = lax.axis_index("tm")
        ps = path_phases(phase_ref, t)
        idx = lax.broadcasted_iota(jnp.int32, (1, PATH), 1)
        offsets = [(t % (8 >> m)) * ROWS - ps[m] for m in range(LEVELS)]
        c, s = lane_turn(idx, offsets)
        table = cos_ref[...] * c - sin_ref[...] * s
        e = dot32(table, n_ref[...], 1, 0)
        hi, lo = split(e)
        e_ref[:, :PATH] = hi
        e_ref[:, PATH:] = lo

    yh, yl = split(y_ref[...])
    e = e_ref[...]
    fit = dot(e, jnp.concatenate([yh, yh], axis=0), ((1,), (0,)))
    fit = fit + dot(e[:, :PATH], yl, ((1,), (0,)))
    o_ref[...] = x_ref[...] - fit


def subtract(phase, cos_r, sin_r, n, x, y):
    tile = 512
    return pl.pallas_call(
        subtract_kernel,
        grid=(COLS // tile,),
        in_specs=[
            pl.BlockSpec(memory_space=pltpu.SMEM),
            pl.BlockSpec((ROWS, PATH), lambda i: (0, 0)),
            pl.BlockSpec((ROWS, PATH), lambda i: (0, 0)),
            pl.BlockSpec((PATH, PATH), lambda i: (0, 0)),
            pl.BlockSpec((ROWS, tile), lambda i: (0, i)),
            pl.BlockSpec((PATH, tile), lambda i: (0, i)),
        ],
        out_specs=pl.BlockSpec((ROWS, tile), lambda i: (0, i)),
        out_shape=jax.ShapeDtypeStruct((ROWS, COLS), f32),
        scratch_shapes=[pltpu.VMEM((ROWS, 2 * PATH), bf16)],
        compiler_params=pltpu.CompilerParams(vmem_limit_bytes=VLIM),
        name="subtract",
    )(phase, cos_r, sin_r, n, x, y)


def body(snapshots, sample_phase):
    cos_r, sin_r, bc, bs, small = make_constants()
    p = project(sample_phase, jnp.asarray(cos_r.T.copy()), jnp.asarray(sin_r.T.copy()), snapshots)
    y = sum_over_time(p)
    f = products(sample_phase, snapshots, y)
    g = gather(f)
    n = solve(sample_phase, jnp.asarray(bc), jnp.asarray(bs), jnp.asarray(small), g)
    return subtract(sample_phase, jnp.asarray(cos_r), jnp.asarray(sin_r), n, snapshots, y)


def solution(mesh):
    return jax.shard_map(
        body,
        mesh=mesh,
        in_specs=(P("tm", "space"), P()),
        out_specs=P("tm", "space"),
        check_vma=False,
    )
```

```python
import functools
import math

import jax
import jax.numpy as jnp
import numpy as np
from jax import lax
from jax.experimental import pallas as pl
from jax.experimental.pallas import tpu as pltpu
from jax.sharding import PartitionSpec as P

NSUB = 256
RANK = 32
LEVELS = 4
PATH = RANK * LEVELS
ROWS = 512
COLS = 3072
HALF = COLS // 2
PIECE = HALF // 4
CHUNKS = 32
STEP = 512
MESH = pl.DeviceIdType.MESH
f32 = jnp.float32
bf16 = jnp.bfloat16
VLIM = 60 * 1024 * 1024


def make_constants():
    j = np.arange(RANK)
    cj = np.where(j == 0, math.sqrt(1.0 / NSUB), math.sqrt(2.0 / NSUB))
    r = np.arange(ROWS)[:, None]
    cos_rows, sin_rows = [], []
    for m in range(LEVELS):
        s = 16 >> m
        ang = math.pi * j * (r + s / 2.0) / (256.0 * s)
        cos_rows.append(cj * np.cos(ang))
        sin_rows.append(cj * np.sin(ang))
    cos_rows = np.concatenate(cos_rows, 1).T.astype(np.float32)
    sin_rows = np.concatenate(sin_rows, 1).T.astype(np.float32)
    k = np.arange(NSUB)[:, None]
    bc = np.zeros((3, NSUB, PATH))
    bs = np.zeros((3, NSUB, PATH))
    for l in range(1, LEVELS):
        for m in range(l):
            ang = math.pi * j * (k * 2.0 ** (m - l) + 0.5) / 256.0
            bc[l - 1, :, m * RANK : (m + 1) * RANK] = cj * np.cos(ang)
            bs[l - 1, :, m * RANK : (m + 1) * RANK] = cj * np.sin(ang)
    q = cj * np.cos(math.pi * j * (k + 0.5) / 256.0)
    qpad = np.zeros((NSUB, PATH))
    qpad[:, :RANK] = q
    wq = np.zeros((NSUB, PATH))
    wq[: NSUB - 1, 64:96] = q[1:]
    wq[:, 96:128] = q
    first = np.zeros((NSUB, PATH))
    first[0, 64:96] = q[0]
    small = np.stack([qpad, wq, first]).astype(np.float32)
    return cos_rows, sin_rows, bc.astype(np.float32), bs.astype(np.float32), small


def cos_sin(num, period):
    frac = num.astype(f32) * (1.0 / period.astype(f32))
    quarter = jnp.floor(frac * 4.0 + 0.5)
    a = (frac - quarter * 0.25) * (2.0 * math.pi)
    a2 = a * a
    c = 1.0 + a2 * (-0.5 + a2 * (1 / 24.0 + a2 * (-1 / 720.0 + a2 * (1 / 40320.0))))
    s = a * (1.0 + a2 * (-1 / 6.0 + a2 * (1 / 120.0 + a2 * (-1 / 5040.0 + a2 * (1 / 362880.0)))))
    qi = quarter.astype(jnp.int32) & 3
    cosv = jnp.where(qi == 0, c, jnp.where(qi == 1, -s, jnp.where(qi == 2, -c, s)))
    sinv = jnp.where(qi == 0, s, jnp.where(qi == 1, c, jnp.where(qi == 2, -s, -c)))
    return cosv, sinv


def path_phases(phase_ref, t):
    return [phase_ref[m, t // (8 >> m)] for m in range(LEVELS)]


def pick(level, values):
    out = jnp.where(level == 0, values[0], values[1])
    out = jnp.where(level == 2, values[2], out)
    return jnp.where(level == 3, values[3], out)


def lane_turn(idx, offsets):
    level, j = idx // RANK, idx % RANK
    period = pick(level, [512 * 16, 512 * 8, 512 * 4, 512 * 2])
    num = (j * pick(level, offsets)) & (period - 1)
    return cos_sin(num, period)


def split(x):
    hi = x.astype(bf16)
    lo = (x - hi.astype(f32)).astype(bf16)
    return hi, lo


def dot(a, b, dims):
    return lax.dot_general(a, b, (dims, ((), ())), preferred_element_type=f32)


def dot32(a, b, ca, cb):
    return lax.dot_general(
        a, b, (((ca,), (cb,)), ((), ())), precision=lax.Precision.HIGHEST, preferred_element_type=f32
    )


def remote(src, dst, send, recv, where):
    return pltpu.make_async_remote_copy(
        src_ref=src, dst_ref=dst, send_sem=send, recv_sem=recv, device_id=where, device_id_type=MESH
    )


def eliminate(a, b):
    block = 8
    sub = lax.broadcasted_iota(jnp.int32, (RANK, 1), 0)
    mats = [a, b]
    for k0 in range(0, RANK, block):
        cols = [
            [jnp.broadcast_to(m[:, k0 + i : k0 + i + 1], (RANK, PATH)) for i in range(block)]
            for m in mats
        ]
        for i in range(block):
            k = k0 + i
            for v in range(2):
                ci = cols[v][i]
                inv = 1.0 / ci[k : k + 1]
                top = mats[v][k : k + 1] * inv
                for j in range(i + 1, block):
                    cj = cols[v][j]
                    sc = cj[k : k + 1] * inv
                    cols[v][j] = jnp.where(sub == k, sc, cj - ci * sc)
                mats[v] = jnp.where(sub == k, top, mats[v] - ci * top)
    return mats[0], mats[1]


def fit_kernel(
    phase_ref, x_hbm, cos_hbm, sin_hbm, bc_hbm, bs_hbm, small_hbm, n_ref, y_hbm,
    xs, ys, p, r1, sb, r2, r3, cs, bcs, bss, small_ref, acc, fa, fb,
    rya, ryb, qa, qb, rza, rzb, xb, cb, gc, gb, gt, lv, tab, fold, xsem, csem, ssem, rsem,
):
    s = lax.axis_index("space")
    t = lax.axis_index("tm")
    yy, zz = s // 8, s % 8
    x, h = t // 2, t % 2
    ps = path_phases(phase_ref, t)
    y_to = [lax.rem(yy + d, 4) for d in range(1, 4)]
    z_to = [lax.rem(zz + d, 8) for d in range(1, 8)]
    dev_y = [{"space": v * 8 + zz} for v in y_to]
    dev_z = [{"space": yy * 8 + v} for v in z_to]
    dev_t = [{"tm": lax.rem(t + d, 8)} for d in range(1, 8)]
    partner = {"tm": x * 2 + 1 - h}
    across = [{"tm": lax.rem(x + d, 4) * 2 + h} for d in range(1, 4)]
    pair_x = {"tm": (x + 1 - 2 * (x % 2)) * 2 + h}

    barrier = pltpu.get_barrier_semaphore()
    for dev in dev_y + dev_z + dev_t:
        pl.semaphore_signal(barrier, inc=1, device_id=dev, device_id_type=MESH)

    mine = pl.multiple_of(h * HALF, 128)
    other = pl.multiple_of((1 - h) * HALF, 128)
    own = pl.ds(mine, HALF)
    spans = [pl.ds(pl.multiple_of(base + i * STEP, 128), STEP) for base in (other, mine) for i in range(3)]
    consts = [
        pltpu.make_async_copy(src, dst, csem.at[i])
        for i, (src, dst) in enumerate(
            [(cos_hbm, cs.at[0]), (sin_hbm, cs.at[1]), (bc_hbm, bcs), (bs_hbm, bss), (small_hbm, small_ref)]
        )
    ]
    loads = [pltpu.make_async_copy(x_hbm.at[:, sp], xs.at[:, sp], xsem.at[i]) for i, sp in enumerate(spans)]
    consts[0].start()
    consts[1].start()
    for c in loads:
        c.start()
    for c in consts[2:]:
        c.start()

    live = []
    count = [0]

    def go(src, dst, where):
        i = count[0]
        count[0] += 1
        c = remote(src, dst, ssem.at[i], rsem.at[i], where)
        c.start()
        live.append(c)
        return c

    def rows(start, n):
        return pl.ds(pl.multiple_of(start, 8), n)

    idx = lax.broadcasted_iota(jnp.int32, (PATH, 1), 0)
    cv, sv = lane_turn(idx, [(t % (8 >> m)) * ROWS - ps[m] for m in range(LEVELS)])
    r = lax.broadcasted_iota(jnp.int32, (PATH, ROWS), 1)
    level = idx // RANK
    on = ((r - pick(level, ps)) & (pick(level, [16, 8, 4, 2]) - 1)) == 0
    consts[0].wait()
    consts[1].wait()
    dh, dl = split(jnp.where(on, cs[0] * cv - cs[1] * sv, 0.0))
    dboth = jnp.concatenate([dh, dl], axis=0)

    def project(i):
        loads[i].wait()
        xh, xl = split(xs[:, spans[i]])
        a = dot(dboth, xh, ((1,), (0,)))
        b = dot(dh, xl, ((1,), (0,)))
        return a[:PATH] + (a[PATH:] + b)

    first = []
    for i in range(3):
        v = project(i)
        p[:, i * STEP : (i + 1) * STEP] = v[: 3 * RANK]
        ys[96:128, spans[i]] = v[3 * RANK :]
        if i == 0:
            pl.semaphore_wait(barrier, 17)
        part = pl.ds(i * STEP, STEP)
        first.append(go(p.at[:, part], r1.at[:, part], partner))
    for i in range(3):
        v = project(3 + i)
        ys[96:128, spans[3 + i]] = v[3 * RANK :]
        part = pl.ds(i * STEP, STEP)
        first[i].wait_recv()
        sb[:, part] = v[: 3 * RANK] + r1[:, part]
    spread = []
    for d in range(1, 4):
        col = pl.ds(pl.multiple_of(lax.rem(x + d, 4) * PIECE, 128), PIECE)
        spread.append(go(sb.at[0:32, col], r3.at[d - 1], across[d - 1]))
    swap = go(sb.at[32:64, :], r2, pair_x)
    ys[64:96, own] = sb[64:96, :]
    later = [go(ys.at[64:96, own], ys.at[64:96, own], partner)]
    for c in spread:
        c.wait_recv()
    spot = pl.ds(pl.multiple_of(mine + x * PIECE, 128), PIECE)
    here = pl.ds(pl.multiple_of(x * PIECE, 128), PIECE)
    ys[0:32, spot] = (sb[0:32, here] + r3[0]) + (r3[1] + r3[2])
    place = ys.at[0:32, spot]
    back = [go(place, place, across[d - 1]) for d in range(1, 4)]
    later.append(go(place, place, partner))
    swap.wait_recv()
    ys[32:64, own] = sb[32:64, :] + r2[...]
    later.append(go(ys.at[32:64, own], ys.at[32:64, own], partner))
    for d in range(1, 4):
        back[d - 1].wait_recv()
        got = pl.ds(pl.multiple_of(mine + lax.rem(x + 4 - d, 4) * PIECE, 128), PIECE)
        later.append(go(ys.at[0:32, got], ys.at[0:32, got], partner))
    for c in later:
        c.wait_recv()
    y_copy = pltpu.make_async_copy(ys, y_hbm, csem.at[5])
    y_copy.start()

    total = None
    for i in range(6):
        part = slice(i * STEP, (i + 1) * STEP)
        xh, xl = split(xs[:, part])
        yh, yl = split(ys[:, part])
        a = dot(xh, jnp.concatenate([yh, yl], axis=0), ((1,), (1,)))
        b = dot(xl, yh, ((1,), (1,)))
        new = a[:, :PATH] + (a[:, PATH:] + b)
        if i == 0:
            acc[...] = new
        else:
            acc[...] += new
    row = 0
    for l in (2, 1, 0):
        for e in range(1 << l):
            fa[pl.ds(row, CHUNKS, stride=8), :] = acc[pl.ds(ps[l] + e * (16 >> l), CHUNKS, stride=16), :]
            row += 1
    fa[pl.ds(row, CHUNKS, stride=8), :] = jnp.zeros((CHUNKS, PATH), f32)

    def spread_y(src, dst):
        return [go(src.at[rows(y_to[d] * 64, 64)], dst.at[d], dev_y[d]) for d in range(3)]

    def spread_z(src, dst):
        return [go(src.at[rows(z_to[d] * 8, 8)], dst.at[d], dev_z[d]) for d in range(7)]

    def send_z(buf):
        piece = buf.at[rows(s * 8, 8)]
        return [go(piece, piece, dev_z[d]) for d in range(7)]

    def send_y(buf):
        band = buf.at[rows(yy * 64, 64)]
        return [go(band, band, dev_y[d]) for d in range(3)]

    def arrive(copies):
        for c in copies:
            c.wait_recv()

    def sum_y(src, got, dst):
        dst[...] = (src[rows(yy * 64, 64), :] + got[0]) + (got[1] + got[2])

    def sum_z(src, got):
        v = [src[rows(zz * 8, 8), :]] + [got[d] for d in range(7)]
        return ((v[0] + v[1]) + (v[2] + v[3])) + ((v[4] + v[5]) + (v[6] + v[7]))

    a1 = spread_y(fa, rya)
    for e in range(8):
        fb[pl.ds(e, CHUNKS, stride=8), :] = acc[pl.ds(ps[3] + 2 * e, CHUNKS, stride=16), :]
    b1 = spread_y(fb, ryb)

    for c in consts[2:]:
        c.wait()
    lane = lax.broadcasted_iota(jnp.int32, (1, PATH), 1)
    rowi = lax.broadcasted_iota(jnp.int32, (NSUB, 1), 0)
    qpad = small_ref[0]
    for l in range(1, LEVELS):
        start = (t // (8 >> l)) * (ROWS * (8 >> l)) + ps[l]
        cv, sv = lane_turn(lane, [start - (t // (8 >> m)) * (ROWS * (8 >> m)) - ps[m] for m in range(LEVELS)])
        table = bcs[l - 1] * cv - bss[l - 1] * sv
        tab[l - 1] = table
        fold[l - 1] = dot32(qpad, table, 0, 0)[:RANK]

    arrive(a1)
    sum_y(fa, rya, qa)
    a2 = spread_z(qa, rza)
    arrive(b1)
    sum_y(fb, ryb, qb)
    b2 = spread_z(qb, rzb)
    arrive(a2)
    xb[t] = sum_z(qa, rza)
    a3 = [go(xb.at[t], xb.at[t], dev_t[d]) for d in range(7)]
    arrive(b2)
    gt[rows(s * 8, 8), :] = sum_z(qb, rzb)
    arrive(a3)
    two = t // 2 * 2
    quad = t // 4 * 4
    for i in range(4):
        cb[2 * i : 2 * i + 2, :] = xb[quad + i][4:6]
    for i in range(8):
        cb[8 + i : 9 + i, :] = xb[i][6:7]
    lane8 = lax.broadcasted_iota(jnp.int32, (8, PATH), 1)
    gc[rows(s * 8, 8), :] = jnp.where(lane8 < 64, cb[0:8, :], pltpu.roll(cb[8:16, :], 64, 1))
    c4 = send_z(gc)
    gb[rows(s * 8, 8), :] = jnp.concatenate([xb[two][0:4], xb[two + 1][0:4]], axis=0)
    b4 = send_z(gb)
    t4 = send_z(gt)
    arrive(c4)
    c5 = send_y(gc)
    arrive(b4)
    b5 = send_y(gb)
    arrive(t4)
    t5 = send_y(gt)

    sub = lax.broadcasted_iota(jnp.int32, (RANK, PATH), 0)
    lan = lax.broadcasted_iota(jnp.int32, (RANK, PATH), 1)
    eye = (sub == lan).astype(f32)
    eye_next = (sub + RANK == lan).astype(f32)
    rblk = lax.broadcasted_iota(jnp.int32, (PATH, PATH), 0) // RANK
    cblk = lax.broadcasted_iota(jnp.int32, (PATH, PATH), 1) // RANK
    wq = small_ref[1]
    head_q = small_ref[2]
    gram = []

    def take_in(l):
        part = jnp.where(lane < RANK * (l + 1), lv[l], 0.0)
        gram.append(dot32(qpad, part, 0, 0)[:RANK])
        return part

    def whole_gram():
        rest = PATH - RANK * len(gram)
        low = jnp.concatenate(gram + ([jnp.zeros((rest, PATH), f32)] if rest else []), axis=0)
        return jnp.where(cblk <= rblk, low, low.T)

    def level_fit(l, part, n, full):
        comb = (sub + RANK * l == lan).astype(f32)
        if l:
            nk = dot32(n, full, 1, 0)
            comb = comb - dot32(fold[l - 1], n, 1, 0)
            part = part - dot32(tab[l - 1], nk, 1, 0)
        wide = jnp.concatenate([comb, jnp.zeros((PATH - RANK, PATH), f32)], axis=0)
        rt = dot32(part, wide, 1, 1)
        right = (
            jnp.where(rowi < NSUB - 1, rt, 0.0)
            + pltpu.roll(jnp.where(rowi > 0, pltpu.roll(rt, RANK, 1), 0.0), NSUB - 1, 0)
            + wq
        )
        narrow = rt[:, :RANK]
        w = dot32(narrow, right, 0, 0)
        head = dot32(narrow, head_q, 0, 0)
        wt = dot32(qpad[:, :RANK], rt, 0, 0)
        ridge_one = 0.1 / RANK * jnp.sum(w * eye)
        mode = jnp.where(lan < RANK, 0.5 * (pltpu.roll(w, RANK, 1) + wt), 0.0)
        ridge_two = 0.1 / RANK * jnp.sum(mode * eye)
        a, b = eliminate(w + ridge_one * eye, mode + ridge_two * eye + eye_next)
        smooth = head + dot32(w, a, 0, 0)[RANK : 2 * RANK]
        coef = dot32(b, smooth, 0, 0)[RANK : 2 * RANK]
        new = dot32(coef, comb, 0, 0)[64:96]
        n_ref[RANK * l : RANK * (l + 1), :] = new
        if l == LEVELS - 1:
            return None
        before = [n[: RANK * l]] if l else []
        return jnp.concatenate(before + [new, jnp.zeros((PATH - RANK * (l + 1), PATH), f32)], axis=0)

    arrive(c5)
    for i in range(8):
        lv[0, 32 * i : 32 * i + 32, :] = pltpu.roll(gc[pl.ds(i, CHUNKS, stride=8), :], 64, 1)
    for i in range(4):
        for e in range(2):
            lv[1, pl.ds(64 * i + e, CHUNKS, stride=2), :] = gc[pl.ds(2 * i + e, CHUNKS, stride=8), :]
    part0 = take_in(0)
    part1 = take_in(1)
    n = level_fit(0, part0, None, None)
    full = whole_gram()
    arrive(b5)
    for i in range(2):
        for e in range(4):
            lv[2, pl.ds(128 * i + e, CHUNKS, stride=4), :] = gb[pl.ds(4 * i + e, CHUNKS, stride=8), :]
    n = level_fit(1, part1, n, full)
    part2 = take_in(2)
    full = whole_gram()
    arrive(t5)
    lv[3] = gt[...]
    n = level_fit(2, part2, n, full)
    part3 = take_in(3)
    level_fit(3, part3, n, whole_gram())
    y_copy.wait()
    for c in live:
        c.wait_send()


N_COPIES = 17 + 2 * 3 + 2 * 7 + 7 + 3 * 7 + 3 * 3


def fit(phase, x, cos_t, sin_t, bc, bs, small):
    hbm = pl.BlockSpec(memory_space=pl.ANY)
    vm = pl.BlockSpec(memory_space=pltpu.VMEM)
    return pl.pallas_call(
        fit_kernel,
        in_specs=[pl.BlockSpec(memory_space=pltpu.SMEM)] + [hbm] * 6,
        out_specs=(vm, hbm),
        out_shape=(
            jax.ShapeDtypeStruct((PATH, PATH), f32),
            jax.ShapeDtypeStruct((PATH, COLS), f32),
        ),
        scratch_shapes=[
            pltpu.VMEM((ROWS, COLS), f32),
            pltpu.VMEM((PATH, COLS), f32),
            pltpu.VMEM((3 * RANK, HALF), f32),
            pltpu.VMEM((3 * RANK, HALF), f32),
            pltpu.VMEM((3 * RANK, HALF), f32),
            pltpu.VMEM((RANK, HALF), f32),
            pltpu.VMEM((3, RANK, PIECE), f32),
            pltpu.VMEM((2, PATH, ROWS), f32),
            pltpu.VMEM((3, NSUB, PATH), f32),
            pltpu.VMEM((3, NSUB, PATH), f32),
            pltpu.VMEM((3, NSUB, PATH), f32),
            pltpu.VMEM((ROWS, PATH), f32),
            pltpu.VMEM((NSUB, PATH), f32),
            pltpu.VMEM((NSUB, PATH), f32),
            pltpu.VMEM((3, 64, PATH), f32),
            pltpu.VMEM((3, 64, PATH), f32),
            pltpu.VMEM((64, PATH), f32),
            pltpu.VMEM((64, PATH), f32),
            pltpu.VMEM((7, 8, PATH), f32),
            pltpu.VMEM((7, 8, PATH), f32),
            pltpu.VMEM((8, 8, PATH), f32),
            pltpu.VMEM((16, PATH), f32),
            pltpu.VMEM((NSUB, PATH), f32),
            pltpu.VMEM((NSUB, PATH), f32),
            pltpu.VMEM((NSUB, PATH), f32),
            pltpu.VMEM((LEVELS, NSUB, PATH), f32),
            pltpu.VMEM((3, NSUB, PATH), f32),
            pltpu.VMEM((3, RANK, PATH), f32),
            pltpu.SemaphoreType.DMA((6,)),
            pltpu.SemaphoreType.DMA((6,)),
            pltpu.SemaphoreType.DMA((N_COPIES,)),
            pltpu.SemaphoreType.DMA((N_COPIES,)),
        ],
        compiler_params=pltpu.CompilerParams(
            collective_id=0, has_side_effects=True, vmem_limit_bytes=VLIM
        ),
        name="fit",
    )(phase, x, cos_t, sin_t, bc, bs, small)


def subtract_kernel(phase_ref, cos_hbm, sin_hbm, n_hbm, x_hbm, y_hbm, o_hbm, cs, ns, xs, ys, csem, xsem, ysem, osem):
    consts = [
        pltpu.make_async_copy(src, dst, csem.at[i])
        for i, (src, dst) in enumerate([(cos_hbm, cs.at[0]), (sin_hbm, cs.at[1]), (n_hbm, ns)])
    ]
    parts = [pl.ds(i * STEP, STEP) for i in range(6)]
    xl = [pltpu.make_async_copy(x_hbm.at[:, sp], xs.at[:, sp], xsem.at[i]) for i, sp in enumerate(parts)]
    yl = [pltpu.make_async_copy(y_hbm.at[:, sp], ys.at[:, sp], ysem.at[i]) for i, sp in enumerate(parts)]
    ol = [pltpu.make_async_copy(xs.at[:, sp], o_hbm.at[:, sp], osem.at[i]) for i, sp in enumerate(parts)]
    for c in consts:
        c.start()
    for a, b in zip(yl, xl):
        a.start()
        b.start()
    t = lax.axis_index("tm")
    ps = path_phases(phase_ref, t)
    idx = lax.broadcasted_iota(jnp.int32, (PATH, 1), 0)
    c, s = lane_turn(idx, [(t % (8 >> m)) * ROWS - ps[m] for m in range(LEVELS)])
    for v in consts:
        v.wait()
    eh, el = split(dot32(cs[0] * c - cs[1] * s, ns[...], 0, 0))
    e = jnp.concatenate([eh, el], axis=1)
    for i, sp in enumerate(parts):
        yl[i].wait()
        yh, ylo = split(ys[:, sp])
        fit_part = dot(e, jnp.concatenate([yh, yh], axis=0), ((1,), (0,)))
        fit_part = fit_part + dot(eh, ylo, ((1,), (0,)))
        xl[i].wait()
        xs[:, sp] = xs[:, sp] - fit_part
        ol[i].start()
    for c in ol:
        c.wait()


def subtract(phase, cos_t, sin_t, n, x, y):
    hbm = pl.BlockSpec(memory_space=pl.ANY)
    return pl.pallas_call(
        subtract_kernel,
        in_specs=[pl.BlockSpec(memory_space=pltpu.SMEM)] + [hbm] * 5,
        out_specs=hbm,
        out_shape=jax.ShapeDtypeStruct((ROWS, COLS), f32),
        scratch_shapes=[
            pltpu.VMEM((2, PATH, ROWS), f32),
            pltpu.VMEM((PATH, PATH), f32),
            pltpu.VMEM((ROWS, COLS), f32),
            pltpu.VMEM((PATH, COLS), f32),
            pltpu.SemaphoreType.DMA((3,)),
            pltpu.SemaphoreType.DMA((6,)),
            pltpu.SemaphoreType.DMA((6,)),
            pltpu.SemaphoreType.DMA((6,)),
        ],
        compiler_params=pltpu.CompilerParams(vmem_limit_bytes=VLIM),
        name="subtract",
    )(phase, cos_t, sin_t, n, x, y)


def body(snapshots, sample_phase):
    cos_t, sin_t, bc, bs, small = [jnp.asarray(v) for v in make_constants()]
    n, y = fit(sample_phase, snapshots, cos_t, sin_t, bc, bs, small)
    return subtract(sample_phase, cos_t, sin_t, n, snapshots, y)


def solution(mesh):
    return jax.shard_map(
        body,
        mesh=mesh,
        in_specs=(P("tm", "space"), P()),
        out_specs=P("tm", "space"),
        check_vma=False,
    )
```

```python
import functools
import math

import jax
import jax.numpy as jnp
import numpy as np
from jax import lax
from jax.experimental import pallas as pl
from jax.experimental.pallas import tpu as pltpu
from jax.sharding import PartitionSpec as P

NSUB = 256
RANK = 32
LEVELS = 4
PATH = RANK * LEVELS
ROWS = 512
COLS = 3072
HALF = COLS // 2
CHUNKS = 32
STEP = 512
MESH = pl.DeviceIdType.MESH
f32 = jnp.float32
bf16 = jnp.bfloat16
FIT_VMEM = 20 * 1024 * 1024
SUB_VMEM = 10 * 1024 * 1024


def make_constants():
    j = np.arange(RANK)
    cj = np.where(j == 0, math.sqrt(1.0 / NSUB), math.sqrt(2.0 / NSUB))
    r = np.arange(ROWS)[:, None]
    cos_rows, sin_rows = [], []
    for m in range(LEVELS):
        s = 16 >> m
        ang = math.pi * j * (r + s / 2.0) / (256.0 * s)
        cos_rows.append(cj * np.cos(ang))
        sin_rows.append(cj * np.sin(ang))
    cos_rows = np.concatenate(cos_rows, 1).T.astype(np.float32)
    sin_rows = np.concatenate(sin_rows, 1).T.astype(np.float32)
    k = np.arange(NSUB)[:, None]
    bc = np.zeros((3, NSUB, PATH))
    bs = np.zeros((3, NSUB, PATH))
    for l in range(1, LEVELS):
        for m in range(l):
            ang = math.pi * j * (k * 2.0 ** (m - l) + 0.5) / 256.0
            bc[l - 1, :, m * RANK : (m + 1) * RANK] = cj * np.cos(ang)
            bs[l - 1, :, m * RANK : (m + 1) * RANK] = cj * np.sin(ang)
    q = cj * np.cos(math.pi * j * (k + 0.5) / 256.0)
    qpad = np.zeros((NSUB, PATH))
    qpad[:, :RANK] = q
    wq = np.zeros((NSUB, PATH))
    wq[: NSUB - 1, 64:96] = q[1:]
    wq[:, 96:128] = q
    first = np.zeros((NSUB, PATH))
    first[0, 64:96] = q[0]
    small = np.stack([qpad, wq, first]).astype(np.float32)
    return cos_rows, sin_rows, bc.astype(np.float32), bs.astype(np.float32), small


def cos_sin(num, period):
    frac = num.astype(f32) * (1.0 / period.astype(f32))
    quarter = jnp.floor(frac * 4.0 + 0.5)
    a = (frac - quarter * 0.25) * (2.0 * math.pi)
    a2 = a * a
    c = 1.0 + a2 * (-0.5 + a2 * (1 / 24.0 + a2 * (-1 / 720.0 + a2 * (1 / 40320.0))))
    s = a * (1.0 + a2 * (-1 / 6.0 + a2 * (1 / 120.0 + a2 * (-1 / 5040.0 + a2 * (1 / 362880.0)))))
    qi = quarter.astype(jnp.int32) & 3
    cosv = jnp.where(qi == 0, c, jnp.where(qi == 1, -s, jnp.where(qi == 2, -c, s)))
    sinv = jnp.where(qi == 0, s, jnp.where(qi == 1, c, jnp.where(qi == 2, -s, -c)))
    return cosv, sinv


def path_phases(phase_ref, t):
    return [phase_ref[m, t // (8 >> m)] for m in range(LEVELS)]


def pick(level, values):
    out = jnp.where(level == 0, values[0], values[1])
    out = jnp.where(level == 2, values[2], out)
    return jnp.where(level == 3, values[3], out)


def lane_turn(idx, offsets):
    level, j = idx // RANK, idx % RANK
    period = pick(level, [512 * 16, 512 * 8, 512 * 4, 512 * 2])
    num = (j * pick(level, offsets)) & (period - 1)
    return cos_sin(num, period)


def split(x):
    hi = x.astype(bf16)
    lo = (x - hi.astype(f32)).astype(bf16)
    return hi, lo


def dot(a, b, dims):
    return lax.dot_general(a, b, (dims, ((), ())), preferred_element_type=f32)


def dot32(a, b, ca, cb):
    return lax.dot_general(
        a, b, (((ca,), (cb,)), ((), ())), precision=lax.Precision.HIGHEST, preferred_element_type=f32
    )


def remote(src, dst, send, recv, where):
    return pltpu.make_async_remote_copy(
        src_ref=src, dst_ref=dst, send_sem=send, recv_sem=recv, device_id=where, device_id_type=MESH
    )


def eliminate(a, b):
    block = 8
    sub = lax.broadcasted_iota(jnp.int32, (RANK, 1), 0)
    mats = [a, b]
    for k0 in range(0, RANK, block):
        cols = [
            [jnp.broadcast_to(m[:, k0 + i : k0 + i + 1], (RANK, PATH)) for i in range(block)]
            for m in mats
        ]
        for i in range(block):
            k = k0 + i
            for v in range(2):
                ci = cols[v][i]
                inv = 1.0 / ci[k : k + 1]
                top = mats[v][k : k + 1] * inv
                for j in range(i + 1, block):
                    cj = cols[v][j]
                    sc = cj[k : k + 1] * inv
                    cols[v][j] = jnp.where(sub == k, sc, cj - ci * sc)
                mats[v] = jnp.where(sub == k, top, mats[v] - ci * top)
    return mats[0], mats[1]


def fit_kernel(
    phase_ref, x_hbm, cos_hbm, sin_hbm, bc_hbm, bs_hbm, small_hbm, e_ref, ys, xs,
    p, r1, sb, rn, r2, r3, mb, cs, bcs, bss, small_ref, acc, fa, fb,
    rya, ryb, qa, qb, rza, rzb, xb, cb, gc, gb, gt, lv, tab, tt, xsem, csem, ssem, rsem,
):
    s = lax.axis_index("space")
    t = lax.axis_index("tm")
    x, h = t // 2, t % 2
    ps = path_phases(phase_ref, t)
    yy, zz = s // 8, s % 8
    y_to = [lax.rem(yy + d, 4) for d in range(1, 4)]
    z_to = [lax.rem(zz + d, 8) for d in range(1, 8)]
    dev_y = [{"space": v * 8 + zz} for v in y_to]
    dev_z = [{"space": yy * 8 + v} for v in z_to]
    dev_t = [{"tm": lax.rem(t + d, 8)} for d in range(1, 8)]
    partner = {"tm": x * 2 + 1 - h}
    beside = {"tm": (x + 1 - 2 * (x % 2)) * 2 + h}
    near = {"tm": (3 - x) * 2 + h}

    barrier = pltpu.get_barrier_semaphore()
    for dev in dev_y + dev_z + dev_t:
        pl.semaphore_signal(barrier, inc=1, device_id=dev, device_id_type=MESH)

    mine = pl.multiple_of(h * HALF, 128)
    other = pl.multiple_of((1 - h) * HALF, 128)
    own = [pl.ds(pl.multiple_of(mine + i * STEP, 128), STEP) for i in range(3)]
    far = [pl.ds(pl.multiple_of(other + i * STEP, 128), STEP) for i in range(3)]
    part = [pl.ds(i * STEP, STEP) for i in range(3)]
    order = [far[0], far[1], own[0], far[2], own[1], own[2]]
    consts = [
        pltpu.make_async_copy(src, dst, csem.at[i])
        for i, (src, dst) in enumerate(
            [(cos_hbm, cs.at[0]), (sin_hbm, cs.at[1]), (bc_hbm, bcs), (bs_hbm, bss), (small_hbm, small_ref)]
        )
    ]
    loads = [pltpu.make_async_copy(x_hbm.at[:, sp], xs.at[:, sp], xsem.at[i]) for i, sp in enumerate(order)]
    consts[0].start()
    consts[1].start()
    for c in loads:
        c.start()
    for c in consts[2:]:
        c.start()

    live = []
    count = [0]

    def go(src, dst, where):
        i = count[0]
        count[0] += 1
        c = remote(src, dst, ssem.at[i], rsem.at[i], where)
        c.start()
        live.append(c)
        return c

    def rows(start, n):
        return pl.ds(pl.multiple_of(start, 8), n)

    idx = lax.broadcasted_iota(jnp.int32, (PATH, 1), 0)
    cv, sv = lane_turn(idx, [(t % (8 >> m)) * ROWS - ps[m] for m in range(LEVELS)])
    r = lax.broadcasted_iota(jnp.int32, (PATH, ROWS), 1)
    level = idx // RANK
    on = ((r - pick(level, ps)) & (pick(level, [16, 8, 4, 2]) - 1)) == 0
    consts[0].wait()
    consts[1].wait()
    dh, dl = split(jnp.where(on, cs[0] * cv - cs[1] * sv, 0.0))
    dboth = jnp.concatenate([dh, dl], axis=0)

    def project(i):
        loads[i].wait()
        xh, xl = split(xs[:, order[i]])
        a = dot(dboth, xh, ((1,), (0,)))
        b = dot(dh, xl, ((1,), (0,)))
        return a[:PATH] + (a[PATH:] + b)

    first, cross, swap, later, merge, back = [], [], [], [], [], []

    def send_out(c, i):
        v = project(i)
        p[:, part[c]] = v[: 3 * RANK]
        ys[96:128, far[c]] = v[3 * RANK :]
        if c == 0:
            pl.semaphore_wait(barrier, 17)
        first.append(go(p.at[:, part[c]], r1.at[:, part[c]], partner))

    def keep(c, i):
        v = project(i)
        sb[:, part[c]] = v[: 3 * RANK]
        ys[96:128, own[c]] = v[3 * RANK :]

    block = x // 2
    mine_blk = [pl.ds(pl.multiple_of(c * STEP + block * 256, 128), 256) for c in range(3)]
    away_blk = [pl.ds(pl.multiple_of(c * STEP + (1 - block) * 256, 128), 256) for c in range(3)]
    place_blk = [pl.ds(pl.multiple_of(mine + c * STEP + block * 256, 128), 256) for c in range(3)]

    def step_one(c):
        first[c].wait_recv()
        sb[:, part[c]] = sb[:, part[c]] + r1[:, part[c]]
        cross.append(go(sb.at[0:32, away_blk[c]], rn.at[c], near))
        swap.append(go(sb.at[32:64, part[c]], r2.at[c], beside))
        ys[64:96, own[c]] = sb[64:96, part[c]]
        later.append([go(ys.at[64:96, own[c]], ys.at[64:96, own[c]], partner)])

    send_out(0, 0)
    send_out(1, 1)
    keep(0, 2)
    step_one(0)
    send_out(2, 3)
    keep(1, 4)
    step_one(1)
    keep(2, 5)
    step_one(2)
    for c in range(3):
        cross[c].wait_recv()
        mb[c] = sb[0:32, mine_blk[c]] + rn[c]
        merge.append(go(mb.at[c], r3.at[c], beside))
    for c in range(3):
        swap[c].wait_recv()
        ys[32:64, own[c]] = sb[32:64, part[c]] + r2[c]
        later[c].append(go(ys.at[32:64, own[c]], ys.at[32:64, own[c]], partner))
        merge[c].wait_recv()
        ys[0:32, place_blk[c]] = mb[c] + r3[c]
        back.append(go(ys.at[0:32, place_blk[c]], ys.at[0:32, place_blk[c]], near))
    for c in range(3):
        back[c].wait_recv()
        later[c].append(go(ys.at[0:32, own[c]], ys.at[0:32, own[c]], partner))

    def product(sp):
        xh, xl = split(xs[:, sp])
        yh, yl = split(ys[:, sp])
        a = dot(xh, jnp.concatenate([yh, yl], axis=0), ((1,), (1,)))
        b = dot(xl, yh, ((1,), (1,)))
        return a[:, :PATH] + (a[:, PATH:] + b)

    acc[...] = product(own[0])
    acc[...] += product(own[1])
    acc[...] += product(own[2])
    for c in range(3):
        for v in later[c]:
            v.wait_recv()
        acc[...] += product(far[c])
    row = 0
    for l in (2, 1, 0):
        for e in range(1 << l):
            fa[pl.ds(row, CHUNKS, stride=8), :] = acc[pl.ds(ps[l] + e * (16 >> l), CHUNKS, stride=16), :]
            row += 1
    fa[pl.ds(row, CHUNKS, stride=8), :] = jnp.zeros((CHUNKS, PATH), f32)

    def spread_y(src, dst):
        return [go(src.at[rows(y_to[d] * 64, 64)], dst.at[d], dev_y[d]) for d in range(3)]

    def spread_z(src, dst):
        return [go(src.at[rows(z_to[d] * 8, 8)], dst.at[d], dev_z[d]) for d in range(7)]

    def send_z(buf):
        piece = buf.at[rows(s * 8, 8)]
        return [go(piece, piece, dev_z[d]) for d in range(7)]

    def send_y(buf):
        band = buf.at[rows(yy * 64, 64)]
        return [go(band, band, dev_y[d]) for d in range(3)]

    def arrive(copies):
        for c in copies:
            c.wait_recv()

    def sum_y(src, got, dst):
        dst[...] = (src[rows(yy * 64, 64), :] + got[0]) + (got[1] + got[2])

    def sum_z(src, got):
        v = [src[rows(zz * 8, 8), :]] + [got[d] for d in range(7)]
        return ((v[0] + v[1]) + (v[2] + v[3])) + ((v[4] + v[5]) + (v[6] + v[7]))

    a1 = spread_y(fa, rya)
    for e in range(8):
        fb[pl.ds(e, CHUNKS, stride=8), :] = acc[pl.ds(ps[3] + 2 * e, CHUNKS, stride=16), :]
    b1 = spread_y(fb, ryb)

    for c in consts[2:]:
        c.wait()
    lane = lax.broadcasted_iota(jnp.int32, (1, PATH), 1)
    rowi = lax.broadcasted_iota(jnp.int32, (NSUB, 1), 0)
    qpad = small_ref[0]
    for l in range(1, LEVELS):
        start = (t // (8 >> l)) * (ROWS * (8 >> l)) + ps[l]
        ca, sa = lane_turn(lane, [start - (t // (8 >> m)) * (ROWS * (8 >> m)) - ps[m] for m in range(LEVELS)])
        table = bcs[l - 1] * ca - bss[l - 1] * sa
        tab[l - 1, 0:NSUB, :] = table
        tab[l - 1, NSUB:, :] = dot32(qpad, table, 0, 0)[:RANK]
    tt[...] = (cs[0] * cv - cs[1] * sv).T

    arrive(a1)
    sum_y(fa, rya, qa)
    a2 = spread_z(qa, rza)
    arrive(b1)
    sum_y(fb, ryb, qb)
    b2 = spread_z(qb, rzb)
    arrive(a2)
    xb[t] = sum_z(qa, rza)
    a3 = [go(xb.at[t], xb.at[t], dev_t[d]) for d in range(7)]
    arrive(b2)
    gt[rows(s * 8, 8), :] = sum_z(qb, rzb)
    arrive(a3)
    two = t // 2 * 2
    quad = t // 4 * 4
    for i in range(4):
        cb[2 * i : 2 * i + 2, :] = xb[quad + i][4:6]
    for i in range(8):
        cb[8 + i : 9 + i, :] = xb[i][6:7]
    lane8 = lax.broadcasted_iota(jnp.int32, (8, PATH), 1)
    gc[rows(s * 8, 8), :] = jnp.where(lane8 < 64, cb[0:8, :], pltpu.roll(cb[8:16, :], 64, 1))
    c4 = send_z(gc)
    gb[rows(s * 8, 8), :] = jnp.concatenate([xb[two][0:4], xb[two + 1][0:4]], axis=0)
    b4 = send_z(gb)
    t4 = send_z(gt)
    arrive(c4)
    c5 = send_y(gc)
    arrive(b4)
    b5 = send_y(gb)
    arrive(t4)
    t5 = send_y(gt)

    sub = lax.broadcasted_iota(jnp.int32, (RANK, PATH), 0)
    lan = lax.broadcasted_iota(jnp.int32, (RANK, PATH), 1)
    eye = (sub == lan).astype(f32)
    eye_next = (sub + RANK == lan).astype(f32)
    rblk = lax.broadcasted_iota(jnp.int32, (PATH, PATH), 0) // RANK
    cblk = lax.broadcasted_iota(jnp.int32, (PATH, PATH), 1) // RANK
    wq = small_ref[1]
    head_q = small_ref[2]
    gram, seen, fits = [], [], []

    def take_in(l):
        v = jnp.where(lane < RANK * (l + 1), lv[l], 0.0)
        seen.append(v)
        gram.append(dot32(qpad, v, 0, 0)[:RANK])

    def fill(blocks):
        rest = PATH - RANK * len(blocks)
        return jnp.concatenate(blocks + ([jnp.zeros((rest, PATH), f32)] if rest else []), axis=0)

    def whole_gram():
        low = fill(gram)
        return jnp.where(cblk <= rblk, low, low.T)

    def level_fit(l, part, comb):
        rt = dot32(part, fill([comb]), 1, 1)
        right = (
            jnp.where(rowi < NSUB - 1, rt, 0.0)
            + pltpu.roll(jnp.where(rowi > 0, pltpu.roll(rt, RANK, 1), 0.0), NSUB - 1, 0)
            + wq
        )
        narrow = rt[:, :RANK]
        w = dot32(narrow, right, 0, 0)
        head = dot32(narrow, head_q, 0, 0)
        wt = dot32(qpad[:, :RANK], rt, 0, 0)
        ridge_one = 0.1 / RANK * jnp.sum(w * eye)
        mode = jnp.where(lan < RANK, 0.5 * (pltpu.roll(w, RANK, 1) + wt), 0.0)
        ridge_two = 0.1 / RANK * jnp.sum(mode * eye)
        a, b = eliminate(w + ridge_one * eye, mode + ridge_two * eye + eye_next)
        smooth = head + dot32(w, a, 0, 0)[RANK : 2 * RANK]
        mc = dot32(b, comb, 0, 0)[RANK : 2 * RANK]
        moved = jnp.where((lan >= 64) & (lan < 96), smooth, 0.0)
        if l != 2:
            moved = pltpu.roll(moved, (RANK * l - 64) % PATH, 1)
        fits.append(dot32(moved, mc, 0, 0)[RANK * l : RANK * (l + 1)])
        return moved, mc

    def advance(l, moved, mc):
        full = whole_gram()
        both = tab[l - 1]
        lead = dot32(both, moved, 1, 1)
        comb = (sub + RANK * l == lan).astype(f32) - dot32(lead[NSUB:], mc, 1, 0)
        part = seen[l] - dot32(lead[:NSUB], dot32(mc, full, 1, 0), 1, 0)
        if l > 1:
            n = fill(fits[: l - 1])
            comb = comb - dot32(both[NSUB:], n, 1, 0)
            part = part - dot32(both[:NSUB], dot32(n, full, 1, 0), 1, 0)
        return part, comb

    arrive(c5)
    for i in range(8):
        lv[0, 32 * i : 32 * i + 32, :] = pltpu.roll(gc[pl.ds(i, CHUNKS, stride=8), :], 64, 1)
    for i in range(4):
        for e in range(2):
            lv[1, pl.ds(64 * i + e, CHUNKS, stride=2), :] = gc[pl.ds(2 * i + e, CHUNKS, stride=8), :]
    take_in(0)
    take_in(1)
    moved, mc = level_fit(0, seen[0], eye)
    nxt = advance(1, moved, mc)
    arrive(b5)
    for i in range(2):
        for e in range(4):
            lv[2, pl.ds(128 * i + e, CHUNKS, stride=4), :] = gb[pl.ds(4 * i + e, CHUNKS, stride=8), :]
    take_in(2)
    moved, mc = level_fit(1, *nxt)
    nxt = advance(2, moved, mc)
    moved, mc = level_fit(2, *nxt)
    arrive(t5)
    lv[3] = gt[...]
    take_in(3)
    nxt = advance(3, moved, mc)
    level_fit(3, *nxt)
    eh, el = split(dot32(tt[...], fill(fits), 1, 0))
    e_ref[:, :PATH] = eh
    e_ref[:, PATH:] = el
    for c in live:
        c.wait_send()


N_COPIES = 24 + 5 * 7 + 5 * 3 + 7


def fit(phase, x, cos_t, sin_t, bc, bs, small):
    hbm = pl.BlockSpec(memory_space=pltpu.HBM)
    vm = pl.BlockSpec(memory_space=pltpu.VMEM)
    return pl.pallas_call(
        fit_kernel,
        in_specs=[pl.BlockSpec(memory_space=pltpu.SMEM)] + [hbm] * 6,
        out_specs=(vm, vm, vm),
        out_shape=(
            jax.ShapeDtypeStruct((ROWS, 2 * PATH), bf16),
            jax.ShapeDtypeStruct((PATH, COLS), f32),
            jax.ShapeDtypeStruct((ROWS, COLS), f32),
        ),
        scratch_shapes=[
            pltpu.VMEM((3 * RANK, HALF), f32),
            pltpu.VMEM((3 * RANK, HALF), f32),
            pltpu.VMEM((3 * RANK, HALF), f32),
            pltpu.VMEM((3, RANK, 256), f32),
            pltpu.VMEM((3, RANK, STEP), f32),
            pltpu.VMEM((3, RANK, 256), f32),
            pltpu.VMEM((3, RANK, 256), f32),
            pltpu.VMEM((2, PATH, ROWS), f32),
            pltpu.VMEM((3, NSUB, PATH), f32),
            pltpu.VMEM((3, NSUB, PATH), f32),
            pltpu.VMEM((3, NSUB, PATH), f32),
            pltpu.VMEM((ROWS, PATH), f32),
            pltpu.VMEM((NSUB, PATH), f32),
            pltpu.VMEM((NSUB, PATH), f32),
            pltpu.VMEM((3, 64, PATH), f32),
            pltpu.VMEM((3, 64, PATH), f32),
            pltpu.VMEM((64, PATH), f32),
            pltpu.VMEM((64, PATH), f32),
            pltpu.VMEM((7, 8, PATH), f32),
            pltpu.VMEM((7, 8, PATH), f32),
            pltpu.VMEM((8, 8, PATH), f32),
            pltpu.VMEM((16, PATH), f32),
            pltpu.VMEM((NSUB, PATH), f32),
            pltpu.VMEM((NSUB, PATH), f32),
            pltpu.VMEM((NSUB, PATH), f32),
            pltpu.VMEM((LEVELS, NSUB, PATH), f32),
            pltpu.VMEM((3, NSUB + RANK, PATH), f32),
            pltpu.VMEM((ROWS, PATH), f32),
            pltpu.SemaphoreType.DMA((6,)),
            pltpu.SemaphoreType.DMA((5,)),
            pltpu.SemaphoreType.DMA((N_COPIES,)),
            pltpu.SemaphoreType.DMA((N_COPIES,)),
        ],
        compiler_params=pltpu.CompilerParams(
            collective_id=0, has_side_effects=True, vmem_limit_bytes=FIT_VMEM
        ),
        name="fit",
    )(phase, x, cos_t, sin_t, bc, bs, small)


def subtract_kernel(e_ref, x_ref, y_ref, o_hbm, rest, osem):
    e = e_ref[...]
    copies = []
    for i in range(6):
        sp = pl.ds(i * STEP, STEP)
        yh, yl = split(y_ref[:, sp])
        fitted = dot(e, jnp.concatenate([yh, yh], axis=0), ((1,), (0,)))
        fitted = fitted + dot(e[:, :PATH], yl, ((1,), (0,)))
        rest[:, sp] = x_ref[:, sp] - fitted
        copies.append(pltpu.make_async_copy(rest.at[:, sp], o_hbm.at[:, sp], osem.at[i]))
        copies[i].start()
    for c in copies:
        c.wait()


def subtract(e, x, y):
    vm = pl.BlockSpec(memory_space=pltpu.VMEM)
    return pl.pallas_call(
        subtract_kernel,
        in_specs=[vm] * 3,
        out_specs=pl.BlockSpec(memory_space=pltpu.HBM),
        out_shape=jax.ShapeDtypeStruct((ROWS, COLS), f32),
        scratch_shapes=[pltpu.VMEM((ROWS, COLS), f32), pltpu.SemaphoreType.DMA((6,))],
        compiler_params=pltpu.CompilerParams(vmem_limit_bytes=SUB_VMEM),
        name="subtract",
    )(e, x, y)


def body(snapshots, sample_phase):
    stay = [
        pltpu.with_memory_space_constraint(v, pltpu.HBM)
        for v in [snapshots] + [jnp.asarray(c) for c in make_constants()]
    ]
    e, y, held = fit(pltpu.with_memory_space_constraint(sample_phase, pltpu.HBM), *stay)
    return subtract(e, held, y)


def solution(mesh):
    return jax.shard_map(
        body,
        mesh=mesh,
        in_specs=(P("tm", "space"), P()),
        out_specs=P("tm", "space"),
        check_vma=False,
    )
```

```python
import functools
import math

import jax
import jax.numpy as jnp
import numpy as np
from jax import lax
from jax.experimental import pallas as pl
from jax.experimental.pallas import tpu as pltpu
from jax.sharding import PartitionSpec as P

NSUB = 256
RANK = 32
LEVELS = 4
PATH = RANK * LEVELS
ROWS = 512
COLS = 3072
HALF = COLS // 2
CHUNKS = 32
STEP = 512
MESH = pl.DeviceIdType.MESH
f32 = jnp.float32
bf16 = jnp.bfloat16
FIT_VMEM = 20 * 1024 * 1024
SUB_VMEM = 10 * 1024 * 1024


def make_constants():
    j = np.arange(RANK)
    cj = np.where(j == 0, math.sqrt(1.0 / NSUB), math.sqrt(2.0 / NSUB))
    r = np.arange(ROWS)[:, None]
    cos_rows, sin_rows = [], []
    for m in range(LEVELS):
        s = 16 >> m
        ang = math.pi * j * (r + s / 2.0) / (256.0 * s)
        cos_rows.append(cj * np.cos(ang))
        sin_rows.append(cj * np.sin(ang))
    cos_rows = np.concatenate(cos_rows, 1).T.astype(np.float32)
    sin_rows = np.concatenate(sin_rows, 1).T.astype(np.float32)
    k = np.arange(NSUB)[:, None]
    bc = np.zeros((3, NSUB, PATH))
    bs = np.zeros((3, NSUB, PATH))
    for l in range(1, LEVELS):
        for m in range(l):
            ang = math.pi * j * (k * 2.0 ** (m - l) + 0.5) / 256.0
            bc[l - 1, :, m * RANK : (m + 1) * RANK] = cj * np.cos(ang)
            bs[l - 1, :, m * RANK : (m + 1) * RANK] = cj * np.sin(ang)
    q = cj * np.cos(math.pi * j * (k + 0.5) / 256.0)
    qpad = np.zeros((NSUB, PATH))
    qpad[:, :RANK] = q
    wq = np.zeros((NSUB, PATH))
    wq[: NSUB - 1, 64:96] = q[1:]
    wq[:, 96:128] = q
    first = np.zeros((NSUB, PATH))
    first[0, 64:96] = q[0]
    small = np.stack([qpad, wq, first]).astype(np.float32)
    return cos_rows, sin_rows, bc.astype(np.float32), bs.astype(np.float32), small


def cos_sin(num, period):
    frac = num.astype(f32) * (1.0 / period.astype(f32))
    quarter = jnp.floor(frac * 4.0 + 0.5)
    a = (frac - quarter * 0.25) * (2.0 * math.pi)
    a2 = a * a
    c = 1.0 + a2 * (-0.5 + a2 * (1 / 24.0 + a2 * (-1 / 720.0 + a2 * (1 / 40320.0))))
    s = a * (1.0 + a2 * (-1 / 6.0 + a2 * (1 / 120.0 + a2 * (-1 / 5040.0 + a2 * (1 / 362880.0)))))
    qi = quarter.astype(jnp.int32) & 3
    cosv = jnp.where(qi == 0, c, jnp.where(qi == 1, -s, jnp.where(qi == 2, -c, s)))
    sinv = jnp.where(qi == 0, s, jnp.where(qi == 1, c, jnp.where(qi == 2, -s, -c)))
    return cosv, sinv


def path_phases(phase_ref, t):
    return [phase_ref[m, t // (8 >> m)] for m in range(LEVELS)]


def pick(level, values):
    out = jnp.where(level == 0, values[0], values[1])
    out = jnp.where(level == 2, values[2], out)
    return jnp.where(level == 3, values[3], out)


def lane_turn(idx, offsets):
    level, j = idx // RANK, idx % RANK
    period = pick(level, [512 * 16, 512 * 8, 512 * 4, 512 * 2])
    num = (j * pick(level, offsets)) & (period - 1)
    return cos_sin(num, period)


def split(x):
    hi = x.astype(bf16)
    lo = (x - hi.astype(f32)).astype(bf16)
    return hi, lo


def dot(a, b, dims):
    return lax.dot_general(a, b, (dims, ((), ())), preferred_element_type=f32)


def dot32(a, b, ca, cb):
    return lax.dot_general(
        a, b, (((ca,), (cb,)), ((), ())), precision=lax.Precision.HIGHEST, preferred_element_type=f32
    )


def dot3(a, b, ca, cb):
    ah, al = split(a)
    bh, bl = split(b)
    dims = ((ca,), (cb,))
    return dot(ah, bh, dims) + (dot(ah, bl, dims) + dot(al, bh, dims))


def remote(src, dst, send, recv, where):
    return pltpu.make_async_remote_copy(
        src_ref=src, dst_ref=dst, send_sem=send, recv_sem=recv, device_id=where, device_id_type=MESH
    )


def eliminate(a, b):
    block = 8
    sub = lax.broadcasted_iota(jnp.int32, (RANK, 1), 0)
    mats = [a, b]
    for k0 in range(0, RANK, block):
        cols = [
            [jnp.broadcast_to(m[:, k0 + i : k0 + i + 1], (RANK, PATH)) for i in range(block)]
            for m in mats
        ]
        for i in range(block):
            k = k0 + i
            for v in range(2):
                ci = cols[v][i]
                inv = 1.0 / ci[k : k + 1]
                top = mats[v][k : k + 1] * inv
                for j in range(i + 1, block):
                    cj = cols[v][j]
                    sc = cj[k : k + 1] * inv
                    cols[v][j] = jnp.where(sub == k, sc, cj - ci * sc)
                mats[v] = jnp.where(sub == k, top, mats[v] - ci * top)
    return mats[0], mats[1]


def fit_kernel(
    phase_ref, x_hbm, cos_hbm, sin_hbm, bc_hbm, bs_hbm, small_hbm, e_ref, ys, xs,
    p, r1, sb, rn, r2, r3, mb, cs, bcs, bss, small_ref, acc, fa, fb,
    rya, ryb, qa, qb, rza, rzb, xb, cb, gc, gb, gt, lv, tab, tt, xsem, csem, ssem, rsem,
):
    s = lax.axis_index("space")
    t = lax.axis_index("tm")
    x, h = t // 2, t % 2
    ps = path_phases(phase_ref, t)
    yy, zz = s // 8, s % 8
    y_to = [lax.rem(yy + d, 4) for d in range(1, 4)]
    z_to = [lax.rem(zz + d, 8) for d in range(1, 8)]
    dev_y = [{"space": v * 8 + zz} for v in y_to]
    dev_z = [{"space": yy * 8 + v} for v in z_to]
    dev_t = [{"tm": lax.rem(t + d, 8)} for d in range(1, 8)]
    partner = {"tm": x * 2 + 1 - h}
    beside = {"tm": (x + 1 - 2 * (x % 2)) * 2 + h}
    near = {"tm": (3 - x) * 2 + h}

    barrier = pltpu.get_barrier_semaphore()
    for dev in dev_y + dev_z + dev_t:
        pl.semaphore_signal(barrier, inc=1, device_id=dev, device_id_type=MESH)

    mine = pl.multiple_of(h * HALF, 128)
    other = pl.multiple_of((1 - h) * HALF, 128)
    own = [pl.ds(pl.multiple_of(mine + i * STEP, 128), STEP) for i in range(3)]
    far = [pl.ds(pl.multiple_of(other + i * STEP, 128), STEP) for i in range(3)]
    part = [pl.ds(i * STEP, STEP) for i in range(3)]
    order = [far[0], far[1], own[0], far[2], own[1], own[2]]
    consts = [
        pltpu.make_async_copy(src, dst, csem.at[i])
        for i, (src, dst) in enumerate(
            [(cos_hbm, cs.at[0]), (sin_hbm, cs.at[1]), (bc_hbm, bcs), (bs_hbm, bss), (small_hbm, small_ref)]
        )
    ]
    loads = [pltpu.make_async_copy(x_hbm.at[:, sp], xs.at[:, sp], xsem.at[i]) for i, sp in enumerate(order)]
    consts[0].start()
    consts[1].start()
    for c in loads:
        c.start()
    for c in consts[2:]:
        c.start()

    live = []
    count = [0]

    def go(src, dst, where):
        i = count[0]
        count[0] += 1
        c = remote(src, dst, ssem.at[i], rsem.at[i], where)
        c.start()
        live.append(c)
        return c

    def rows(start, n):
        return pl.ds(pl.multiple_of(start, 8), n)

    idx = lax.broadcasted_iota(jnp.int32, (PATH, 1), 0)
    cv, sv = lane_turn(idx, [(t % (8 >> m)) * ROWS - ps[m] for m in range(LEVELS)])
    r = lax.broadcasted_iota(jnp.int32, (PATH, ROWS), 1)
    level = idx // RANK
    on = ((r - pick(level, ps)) & (pick(level, [16, 8, 4, 2]) - 1)) == 0
    consts[0].wait()
    consts[1].wait()
    dh, dl = split(jnp.where(on, cs[0] * cv - cs[1] * sv, 0.0))
    dboth = jnp.concatenate([dh, dl], axis=0)

    def project(i):
        loads[i].wait()
        xh, xl = split(xs[:, order[i]])
        a = dot(dboth, xh, ((1,), (0,)))
        b = dot(dh, xl, ((1,), (0,)))
        return a[:PATH] + (a[PATH:] + b)

    first, cross, swap, later, merge, back = [], [], [], [], [], []

    def send_out(c, i):
        v = project(i)
        p[:, part[c]] = v[: 3 * RANK]
        ys[96:128, far[c]] = v[3 * RANK :]
        if c == 0:
            pl.semaphore_wait(barrier, 17)
        first.append(go(p.at[:, part[c]], r1.at[:, part[c]], partner))

    def keep(c, i):
        v = project(i)
        sb[:, part[c]] = v[: 3 * RANK]
        ys[96:128, own[c]] = v[3 * RANK :]

    block = x // 2
    mine_blk = [pl.ds(pl.multiple_of(c * STEP + block * 256, 128), 256) for c in range(3)]
    away_blk = [pl.ds(pl.multiple_of(c * STEP + (1 - block) * 256, 128), 256) for c in range(3)]
    place_blk = [pl.ds(pl.multiple_of(mine + c * STEP + block * 256, 128), 256) for c in range(3)]

    def trade(c):
        swap.append(go(sb.at[32:64, part[c]], r2.at[c], beside))

    def step_one(c):
        first[c].wait_recv()
        sb[:, part[c]] = sb[:, part[c]] + r1[:, part[c]]
        cross.append(go(sb.at[0:32, away_blk[c]], rn.at[c], near))
        if c == 0:
            trade(c)
        ys[64:96, own[c]] = sb[64:96, part[c]]
        later.append([go(ys.at[64:96, own[c]], ys.at[64:96, own[c]], partner)])

    send_out(0, 0)
    send_out(1, 1)
    keep(0, 2)
    step_one(0)
    send_out(2, 3)
    keep(1, 4)
    step_one(1)
    keep(2, 5)
    step_one(2)
    for c in range(3):
        cross[c].wait_recv()
        mb[c] = sb[0:32, mine_blk[c]] + rn[c]
        merge.append(go(mb.at[c], r3.at[c], beside))
    trade(1)
    trade(2)
    for c in range(3):
        merge[c].wait_recv()
        ys[0:32, place_blk[c]] = mb[c] + r3[c]
        back.append(go(ys.at[0:32, place_blk[c]], ys.at[0:32, place_blk[c]], near))
    for c in range(3):
        swap[c].wait_recv()
        ys[32:64, own[c]] = sb[32:64, part[c]] + r2[c]
        later[c].append(go(ys.at[32:64, own[c]], ys.at[32:64, own[c]], partner))
    for c in range(3):
        back[c].wait_recv()
        later[c].append(go(ys.at[0:32, own[c]], ys.at[0:32, own[c]], partner))

    def product(sp):
        xh, xl = split(xs[:, sp])
        yh, yl = split(ys[:, sp])
        a = dot(xh, jnp.concatenate([yh, yl], axis=0), ((1,), (1,)))
        b = dot(xl, yh, ((1,), (1,)))
        return a[:, :PATH] + (a[:, PATH:] + b)

    acc[...] = product(own[0])
    acc[...] += product(own[1])
    acc[...] += product(own[2])
    for c in range(3):
        for v in later[c]:
            v.wait_recv()
        acc[...] += product(far[c])
    row = 0
    for l in (2, 1, 0):
        for e in range(1 << l):
            fa[pl.ds(row, CHUNKS, stride=8), :] = acc[pl.ds(ps[l] + e * (16 >> l), CHUNKS, stride=16), :]
            row += 1
    fa[pl.ds(row, CHUNKS, stride=8), :] = jnp.zeros((CHUNKS, PATH), f32)

    def spread_y(src, dst):
        return [go(src.at[rows(y_to[d] * 64, 64)], dst.at[d], dev_y[d]) for d in range(3)]

    def spread_z(src, dst):
        return [go(src.at[rows(z_to[d] * 8, 8)], dst.at[d], dev_z[d]) for d in range(7)]

    def send_z(buf):
        piece = buf.at[rows(s * 8, 8)]
        return [go(piece, piece, dev_z[d]) for d in range(7)]

    def send_y(buf):
        band = buf.at[rows(yy * 64, 64)]
        return [go(band, band, dev_y[d]) for d in range(3)]

    def arrive(copies):
        for c in copies:
            c.wait_recv()

    def sum_y(src, got, dst):
        dst[...] = (src[rows(yy * 64, 64), :] + got[0]) + (got[1] + got[2])

    def sum_z(src, got):
        v = [src[rows(zz * 8, 8), :]] + [got[d] for d in range(7)]
        return ((v[0] + v[1]) + (v[2] + v[3])) + ((v[4] + v[5]) + (v[6] + v[7]))

    a1 = spread_y(fa, rya)
    for e in range(8):
        fb[pl.ds(e, CHUNKS, stride=8), :] = acc[pl.ds(ps[3] + 2 * e, CHUNKS, stride=16), :]
    b1 = spread_y(fb, ryb)

    for c in consts[2:]:
        c.wait()
    lane = lax.broadcasted_iota(jnp.int32, (1, PATH), 1)
    rowi = lax.broadcasted_iota(jnp.int32, (NSUB, 1), 0)
    qpad = small_ref[0]
    for l in range(1, LEVELS):
        start = (t // (8 >> l)) * (ROWS * (8 >> l)) + ps[l]
        ca, sa = lane_turn(lane, [start - (t // (8 >> m)) * (ROWS * (8 >> m)) - ps[m] for m in range(LEVELS)])
        table = bcs[l - 1] * ca - bss[l - 1] * sa
        tab[l - 1, 0:NSUB, :] = table
        tab[l - 1, NSUB:, :] = dot32(qpad, table, 0, 0)[:RANK]
    tt[...] = (cs[0] * cv - cs[1] * sv).T

    arrive(a1)
    sum_y(fa, rya, qa)
    a2 = spread_z(qa, rza)
    arrive(b1)
    sum_y(fb, ryb, qb)
    b2 = spread_z(qb, rzb)
    arrive(a2)
    xb[t] = sum_z(qa, rza)
    a3 = [go(xb.at[t], xb.at[t], dev_t[d]) for d in range(7)]
    arrive(b2)
    gt[rows(s * 8, 8), :] = sum_z(qb, rzb)
    arrive(a3)
    two = t // 2 * 2
    quad = t // 4 * 4
    for i in range(4):
        cb[2 * i : 2 * i + 2, :] = xb[quad + i][4:6]
    for i in range(8):
        cb[8 + i : 9 + i, :] = xb[i][6:7]
    lane8 = lax.broadcasted_iota(jnp.int32, (8, PATH), 1)
    gc[rows(s * 8, 8), :] = jnp.where(lane8 < 64, cb[0:8, :], pltpu.roll(cb[8:16, :], 64, 1))
    c4 = send_z(gc)
    gb[rows(s * 8, 8), :] = jnp.concatenate([xb[two][0:4], xb[two + 1][0:4]], axis=0)
    b4 = send_z(gb)
    t4 = send_z(gt)
    arrive(c4)
    c5 = send_y(gc)
    arrive(b4)
    b5 = send_y(gb)
    arrive(t4)
    t5 = send_y(gt)

    sub = lax.broadcasted_iota(jnp.int32, (RANK, PATH), 0)
    lan = lax.broadcasted_iota(jnp.int32, (RANK, PATH), 1)
    eye = (sub == lan).astype(f32)
    eye_next = (sub + RANK == lan).astype(f32)
    rblk = lax.broadcasted_iota(jnp.int32, (PATH, PATH), 0) // RANK
    cblk = lax.broadcasted_iota(jnp.int32, (PATH, PATH), 1) // RANK
    wq = small_ref[1]
    head_q = small_ref[2]
    gram, seen, fits = [], [], []

    def take_in(l):
        v = jnp.where(lane < RANK * (l + 1), lv[l], 0.0)
        seen.append(v)
        gram.append(dot32(qpad, v, 0, 0)[:RANK])

    def fill(blocks):
        rest = PATH - RANK * len(blocks)
        return jnp.concatenate(blocks + ([jnp.zeros((rest, PATH), f32)] if rest else []), axis=0)

    def whole_gram():
        low = fill(gram)
        return jnp.where(cblk <= rblk, low, low.T)

    def trace(v):
        return jnp.sum(jnp.sum(v * eye, axis=0, keepdims=True), axis=1, keepdims=True)

    def level_fit(l, part, comb):
        rt = dot3(part, fill([comb]), 1, 1) if l else part
        right = (
            jnp.where(rowi < NSUB - 1, rt, 0.0)
            + pltpu.roll(jnp.where(rowi > 0, pltpu.roll(rt, RANK, 1), 0.0), NSUB - 1, 0)
            + wq
        )
        narrow = rt[:, :RANK]
        w = dot32(narrow, right, 0, 0)
        head = dot32(narrow, head_q, 0, 0)
        wt = dot32(qpad[:, :RANK], rt, 0, 0)
        ridge_one = 0.1 / RANK * trace(w)
        mode = jnp.where(lan < RANK, 0.5 * (pltpu.roll(w, RANK, 1) + wt), 0.0)
        ridge_two = 0.1 / RANK * trace(mode)
        a, b = eliminate(w + ridge_one * eye, mode + ridge_two * eye + eye_next)
        smooth = head + dot32(w, a, 0, 0)[RANK : 2 * RANK]
        mc = dot32(b, comb, 0, 0)[RANK : 2 * RANK]
        moved = jnp.where((lan >= 64) & (lan < 96), smooth, 0.0)
        if l != 2:
            moved = pltpu.roll(moved, (RANK * l - 64) % PATH, 1)
        fits.append(dot32(moved, mc, 0, 0)[RANK * l : RANK * (l + 1)])
        return moved, mc

    def advance(l, moved, mc):
        full = whole_gram()
        both = tab[l - 1]
        lead = dot3(both, moved, 1, 1)
        comb = (sub + RANK * l == lan).astype(f32) - dot3(lead[NSUB:], mc, 1, 0)
        part = seen[l] - dot3(lead[:NSUB], dot3(mc, full, 1, 0), 1, 0)
        if l > 1:
            n = fill(fits[: l - 1])
            comb = comb - dot3(both[NSUB:], n, 1, 0)
            part = part - dot3(both[:NSUB], dot3(n, full, 1, 0), 1, 0)
        return part, comb

    arrive(c5)
    for i in range(8):
        lv[0, 32 * i : 32 * i + 32, :] = pltpu.roll(gc[pl.ds(i, CHUNKS, stride=8), :], 64, 1)
    for i in range(4):
        for e in range(2):
            lv[1, pl.ds(64 * i + e, CHUNKS, stride=2), :] = gc[pl.ds(2 * i + e, CHUNKS, stride=8), :]
    take_in(0)
    take_in(1)
    moved, mc = level_fit(0, seen[0], eye)
    nxt = advance(1, moved, mc)
    arrive(b5)
    for i in range(2):
        for e in range(4):
            lv[2, pl.ds(128 * i + e, CHUNKS, stride=4), :] = gb[pl.ds(4 * i + e, CHUNKS, stride=8), :]
    take_in(2)
    moved, mc = level_fit(1, *nxt)
    nxt = advance(2, moved, mc)
    moved, mc = level_fit(2, *nxt)
    arrive(t5)
    lv[3] = gt[...]
    take_in(3)
    nxt = advance(3, moved, mc)
    level_fit(3, *nxt)
    eh, el = split(dot32(tt[...], fill(fits), 1, 0))
    e_ref[:, :PATH] = eh
    e_ref[:, PATH:] = el
    for c in live:
        c.wait_send()


N_COPIES = 24 + 5 * 7 + 5 * 3 + 7


def fit(phase, x, cos_t, sin_t, bc, bs, small):
    hbm = pl.BlockSpec(memory_space=pltpu.HBM)
    vm = pl.BlockSpec(memory_space=pltpu.VMEM)
    return pl.pallas_call(
        fit_kernel,
        in_specs=[pl.BlockSpec(memory_space=pltpu.SMEM)] + [hbm] * 6,
        out_specs=(vm, vm, vm),
        out_shape=(
            jax.ShapeDtypeStruct((ROWS, 2 * PATH), bf16),
            jax.ShapeDtypeStruct((PATH, COLS), f32),
            jax.ShapeDtypeStruct((ROWS, COLS), f32),
        ),
        scratch_shapes=[
            pltpu.VMEM((3 * RANK, HALF), f32),
            pltpu.VMEM((3 * RANK, HALF), f32),
            pltpu.VMEM((3 * RANK, HALF), f32),
            pltpu.VMEM((3, RANK, 256), f32),
            pltpu.VMEM((3, RANK, STEP), f32),
            pltpu.VMEM((3, RANK, 256), f32),
            pltpu.VMEM((3, RANK, 256), f32),
            pltpu.VMEM((2, PATH, ROWS), f32),
            pltpu.VMEM((3, NSUB, PATH), f32),
            pltpu.VMEM((3, NSUB, PATH), f32),
            pltpu.VMEM((3, NSUB, PATH), f32),
            pltpu.VMEM((ROWS, PATH), f32),
            pltpu.VMEM((NSUB, PATH), f32),
            pltpu.VMEM((NSUB, PATH), f32),
            pltpu.VMEM((3, 64, PATH), f32),
            pltpu.VMEM((3, 64, PATH), f32),
            pltpu.VMEM((64, PATH), f32),
            pltpu.VMEM((64, PATH), f32),
            pltpu.VMEM((7, 8, PATH), f32),
            pltpu.VMEM((7, 8, PATH), f32),
            pltpu.VMEM((8, 8, PATH), f32),
            pltpu.VMEM((16, PATH), f32),
            pltpu.VMEM((NSUB, PATH), f32),
            pltpu.VMEM((NSUB, PATH), f32),
            pltpu.VMEM((NSUB, PATH), f32),
            pltpu.VMEM((LEVELS, NSUB, PATH), f32),
            pltpu.VMEM((3, NSUB + RANK, PATH), f32),
            pltpu.VMEM((ROWS, PATH), f32),
            pltpu.SemaphoreType.DMA((6,)),
            pltpu.SemaphoreType.DMA((5,)),
            pltpu.SemaphoreType.DMA((N_COPIES,)),
            pltpu.SemaphoreType.DMA((N_COPIES,)),
        ],
        compiler_params=pltpu.CompilerParams(
            collective_id=0, has_side_effects=True, vmem_limit_bytes=FIT_VMEM
        ),
        name="fit",
    )(phase, x, cos_t, sin_t, bc, bs, small)


def subtract_kernel(e_ref, x_ref, y_ref, o_hbm, rest, osem):
    e = e_ref[...]
    copies = []
    for i in range(6):
        sp = pl.ds(i * STEP, STEP)
        yh, yl = split(y_ref[:, sp])
        fitted = dot(e, jnp.concatenate([yh, yh], axis=0), ((1,), (0,)))
        fitted = fitted + dot(e[:, :PATH], yl, ((1,), (0,)))
        rest[:, sp] = x_ref[:, sp] - fitted
        copies.append(pltpu.make_async_copy(rest.at[:, sp], o_hbm.at[:, sp], osem.at[i]))
        copies[i].start()
    for c in copies:
        c.wait()


def subtract(e, x, y):
    vm = pl.BlockSpec(memory_space=pltpu.VMEM)
    return pl.pallas_call(
        subtract_kernel,
        in_specs=[vm] * 3,
        out_specs=pl.BlockSpec(memory_space=pltpu.HBM),
        out_shape=jax.ShapeDtypeStruct((ROWS, COLS), f32),
        scratch_shapes=[pltpu.VMEM((ROWS, COLS), f32), pltpu.SemaphoreType.DMA((6,))],
        compiler_params=pltpu.CompilerParams(vmem_limit_bytes=SUB_VMEM),
        name="subtract",
    )(e, x, y)


def body(snapshots, sample_phase):
    stay = [
        pltpu.with_memory_space_constraint(v, pltpu.HBM)
        for v in [snapshots] + [jnp.asarray(c) for c in make_constants()]
    ]
    e, y, held = fit(pltpu.with_memory_space_constraint(sample_phase, pltpu.HBM), *stay)
    return subtract(e, held, y)


def solution(mesh):
    return jax.shard_map(
        body,
        mesh=mesh,
        in_specs=(P("tm", "space"), P()),
        out_specs=P("tm", "space"),
        check_vma=False,
    )
```

```python
import functools
import math

import jax
import jax.numpy as jnp
import numpy as np
from jax import lax
from jax.experimental import pallas as pl
from jax.experimental.pallas import tpu as pltpu
from jax.sharding import PartitionSpec as P

NSUB = 256
RANK = 32
LEVELS = 4
PATH = RANK * LEVELS
ROWS = 512
COLS = 3072
HALF = COLS // 2
CHUNKS = 32
STEP = 512
MESH = pl.DeviceIdType.MESH
f32 = jnp.float32
bf16 = jnp.bfloat16
FIT_VMEM = 20 * 1024 * 1024
SUB_VMEM = 10 * 1024 * 1024


def make_constants():
    j = np.arange(RANK)
    cj = np.where(j == 0, math.sqrt(1.0 / NSUB), math.sqrt(2.0 / NSUB))
    r = np.arange(ROWS)[:, None]
    cos_rows, sin_rows = [], []
    for m in range(LEVELS):
        s = 16 >> m
        ang = math.pi * j * (r + s / 2.0) / (256.0 * s)
        cos_rows.append(cj * np.cos(ang))
        sin_rows.append(cj * np.sin(ang))
    cos_rows = np.concatenate(cos_rows, 1).T.astype(np.float32)
    sin_rows = np.concatenate(sin_rows, 1).T.astype(np.float32)
    k = np.arange(NSUB)[:, None]
    bc = np.zeros((3, NSUB, PATH))
    bs = np.zeros((3, NSUB, PATH))
    for l in range(1, LEVELS):
        for m in range(l):
            ang = math.pi * j * (k * 2.0 ** (m - l) + 0.5) / 256.0
            bc[l - 1, :, m * RANK : (m + 1) * RANK] = cj * np.cos(ang)
            bs[l - 1, :, m * RANK : (m + 1) * RANK] = cj * np.sin(ang)
    q = cj * np.cos(math.pi * j * (k + 0.5) / 256.0)
    qpad = np.zeros((NSUB, PATH))
    qpad[:, :RANK] = q
    wq = np.zeros((NSUB, PATH))
    wq[: NSUB - 1, 64:96] = q[1:]
    wq[:, 96:128] = q
    first = np.zeros((NSUB, PATH))
    first[0, 64:96] = q[0]
    small = np.stack([qpad, wq, first]).astype(np.float32)
    return cos_rows, sin_rows, bc.astype(np.float32), bs.astype(np.float32), small


def cos_sin(num, period):
    frac = num.astype(f32) * (1.0 / period.astype(f32))
    quarter = jnp.floor(frac * 4.0 + 0.5)
    a = (frac - quarter * 0.25) * (2.0 * math.pi)
    a2 = a * a
    c = 1.0 + a2 * (-0.5 + a2 * (1 / 24.0 + a2 * (-1 / 720.0 + a2 * (1 / 40320.0))))
    s = a * (1.0 + a2 * (-1 / 6.0 + a2 * (1 / 120.0 + a2 * (-1 / 5040.0 + a2 * (1 / 362880.0)))))
    qi = quarter.astype(jnp.int32) & 3
    cosv = jnp.where(qi == 0, c, jnp.where(qi == 1, -s, jnp.where(qi == 2, -c, s)))
    sinv = jnp.where(qi == 0, s, jnp.where(qi == 1, c, jnp.where(qi == 2, -s, -c)))
    return cosv, sinv


def path_phases(phase_ref, t):
    return [phase_ref[m, t // (8 >> m)] for m in range(LEVELS)]


def pick(level, values):
    out = jnp.where(level == 0, values[0], values[1])
    out = jnp.where(level == 2, values[2], out)
    return jnp.where(level == 3, values[3], out)


def lane_turn(idx, offsets):
    level, j = idx // RANK, idx % RANK
    period = pick(level, [512 * 16, 512 * 8, 512 * 4, 512 * 2])
    num = (j * pick(level, offsets)) & (period - 1)
    return cos_sin(num, period)


def split(x):
    hi = x.astype(bf16)
    lo = (x - hi.astype(f32)).astype(bf16)
    return hi, lo


def dot(a, b, dims):
    return lax.dot_general(a, b, (dims, ((), ())), preferred_element_type=f32)


def dot32(a, b, ca, cb):
    return lax.dot_general(
        a, b, (((ca,), (cb,)), ((), ())), precision=lax.Precision.HIGHEST, preferred_element_type=f32
    )


def dot3(a, b, ca, cb):
    ah, al = split(a)
    bh, bl = split(b)
    dims = ((ca,), (cb,))
    return dot(ah, bh, dims) + (dot(ah, bl, dims) + dot(al, bh, dims))


def remote(src, dst, send, recv, where):
    return pltpu.make_async_remote_copy(
        src_ref=src, dst_ref=dst, send_sem=send, recv_sem=recv, device_id=where, device_id_type=MESH
    )


def eliminate(a, b):
    block = 8
    sub = lax.broadcasted_iota(jnp.int32, (RANK, 1), 0)
    mats = [a, b]
    for k0 in range(0, RANK, block):
        cols = [
            [jnp.broadcast_to(m[:, k0 + i : k0 + i + 1], (RANK, PATH)) for i in range(block)]
            for m in mats
        ]
        for i in range(block):
            k = k0 + i
            for v in range(2):
                ci = cols[v][i]
                inv = 1.0 / ci[k : k + 1]
                top = mats[v][k : k + 1] * inv
                for j in range(i + 1, block):
                    cj = cols[v][j]
                    sc = cj[k : k + 1] * inv
                    cols[v][j] = jnp.where(sub == k, sc, cj - ci * sc)
                mats[v] = jnp.where(sub == k, top, mats[v] - ci * top)
    return mats[0], mats[1]


def fit_kernel(
    phase_ref, x_hbm, cos_hbm, sin_hbm, bc_hbm, bs_hbm, small_hbm, e_ref, ys, xs,
    p, r1, sb, rn, r2, r3, mb, cs, bcs, bss, small_ref, acc, fa, fb,
    rya, ryb, qa, qb, rza, rzb, xb, cb, gc, gb, gt, lv, tab, tt, xsem, csem, ssem, rsem,
):
    s = lax.axis_index("space")
    t = lax.axis_index("tm")
    x, h = t // 2, t % 2
    ps = path_phases(phase_ref, t)
    yy, zz = s // 8, s % 8
    y_to = [lax.rem(yy + d, 4) for d in range(1, 4)]
    z_to = [lax.rem(zz + d, 8) for d in range(1, 8)]
    dev_y = [{"space": v * 8 + zz} for v in y_to]
    dev_z = [{"space": yy * 8 + v} for v in z_to]
    dev_t = [{"tm": lax.rem(t + d, 8)} for d in range(1, 8)]
    partner = {"tm": x * 2 + 1 - h}
    beside = {"tm": (x + 1 - 2 * (x % 2)) * 2 + h}
    near = {"tm": (3 - x) * 2 + h}

    barrier = pltpu.get_barrier_semaphore()
    for dev in dev_y + dev_z + dev_t:
        pl.semaphore_signal(barrier, inc=1, device_id=dev, device_id_type=MESH)

    mine = pl.multiple_of(h * HALF, 128)
    other = pl.multiple_of((1 - h) * HALF, 128)
    own = [pl.ds(pl.multiple_of(mine + i * STEP, 128), STEP) for i in range(3)]
    far = [pl.ds(pl.multiple_of(other + i * STEP, 128), STEP) for i in range(3)]
    part = [pl.ds(i * STEP, STEP) for i in range(3)]
    order = [far[0], far[1], own[0], far[2], own[1], own[2]]
    consts = [
        pltpu.make_async_copy(src, dst, csem.at[i])
        for i, (src, dst) in enumerate(
            [(cos_hbm, cs.at[0]), (sin_hbm, cs.at[1]), (bc_hbm, bcs), (bs_hbm, bss), (small_hbm, small_ref)]
        )
    ]
    loads = [pltpu.make_async_copy(x_hbm.at[:, sp], xs.at[:, sp], xsem.at[i]) for i, sp in enumerate(order)]
    consts[0].start()
    consts[1].start()
    for c in loads:
        c.start()
    for c in consts[2:]:
        c.start()

    live = []
    count = [0]

    def go(src, dst, where):
        i = count[0]
        count[0] += 1
        c = remote(src, dst, ssem.at[i], rsem.at[i], where)
        c.start()
        live.append(c)
        return c

    def rows(start, n):
        return pl.ds(pl.multiple_of(start, 8), n)

    idx = lax.broadcasted_iota(jnp.int32, (PATH, 1), 0)
    cv, sv = lane_turn(idx, [(t % (8 >> m)) * ROWS - ps[m] for m in range(LEVELS)])
    r = lax.broadcasted_iota(jnp.int32, (PATH, ROWS), 1)
    level = idx // RANK
    on = ((r - pick(level, ps)) & (pick(level, [16, 8, 4, 2]) - 1)) == 0
    consts[0].wait()
    consts[1].wait()
    dh, dl = split(jnp.where(on, cs[0] * cv - cs[1] * sv, 0.0))
    dboth = jnp.concatenate([dh, dl], axis=0)

    def project(i):
        loads[i].wait()
        xh, xl = split(xs[:, order[i]])
        a = dot(dboth, xh, ((1,), (0,)))
        b = dot(dh, xl, ((1,), (0,)))
        return a[:PATH] + (a[PATH:] + b)

    first, cross, swap, later, merge, back = [], [], [], [], [], []

    def send_out(c, i):
        v = project(i)
        p[:, part[c]] = v[: 3 * RANK]
        ys[96:128, far[c]] = v[3 * RANK :]
        if c == 0:
            pl.semaphore_wait(barrier, 17)
        first.append(go(p.at[:, part[c]], r1.at[:, part[c]], partner))

    def keep(c, i):
        v = project(i)
        sb[:, part[c]] = v[: 3 * RANK]
        ys[96:128, own[c]] = v[3 * RANK :]

    block = x // 2
    mine_blk = [pl.ds(pl.multiple_of(c * STEP + block * 256, 128), 256) for c in range(3)]
    away_blk = [pl.ds(pl.multiple_of(c * STEP + (1 - block) * 256, 128), 256) for c in range(3)]
    place_blk = [pl.ds(pl.multiple_of(mine + c * STEP + block * 256, 128), 256) for c in range(3)]

    def trade(c):
        swap.append(go(sb.at[32:64, part[c]], r2.at[c], beside))

    def step_one(c):
        first[c].wait_recv()
        sb[:, part[c]] = sb[:, part[c]] + r1[:, part[c]]
        cross.append(go(sb.at[0:32, away_blk[c]], rn.at[c], near))
        if c == 0:
            trade(c)
        ys[64:96, own[c]] = sb[64:96, part[c]]
        later.append([go(ys.at[64:96, own[c]], ys.at[64:96, own[c]], partner)])

    send_out(0, 0)
    send_out(1, 1)
    keep(0, 2)
    step_one(0)
    send_out(2, 3)
    keep(1, 4)
    step_one(1)
    keep(2, 5)
    step_one(2)
    for c in range(3):
        cross[c].wait_recv()
        mb[c] = sb[0:32, mine_blk[c]] + rn[c]
        merge.append(go(mb.at[c], r3.at[c], beside))
    trade(1)
    trade(2)
    for c in range(3):
        merge[c].wait_recv()
        ys[0:32, place_blk[c]] = mb[c] + r3[c]
        back.append(go(ys.at[0:32, place_blk[c]], ys.at[0:32, place_blk[c]], near))
    for c in range(3):
        swap[c].wait_recv()
        ys[32:64, own[c]] = sb[32:64, part[c]] + r2[c]
        later[c].append(go(ys.at[32:64, own[c]], ys.at[32:64, own[c]], partner))
    for c in range(3):
        back[c].wait_recv()
        later[c].append(go(ys.at[0:32, own[c]], ys.at[0:32, own[c]], partner))

    def product(sp):
        xh, xl = split(xs[:, sp])
        yh, yl = split(ys[:, sp])
        a = dot(xh, jnp.concatenate([yh, yl], axis=0), ((1,), (1,)))
        b = dot(xl, yh, ((1,), (1,)))
        return a[:, :PATH] + (a[:, PATH:] + b)

    acc[...] = product(own[0])
    acc[...] += product(own[1])
    acc[...] += product(own[2])
    for c in range(3):
        for v in later[c]:
            v.wait_recv()
        acc[...] += product(far[c])
    row = 0
    for l in (2, 1, 0):
        for e in range(1 << l):
            fa[pl.ds(row, CHUNKS, stride=8), :] = acc[pl.ds(ps[l] + e * (16 >> l), CHUNKS, stride=16), :]
            row += 1
    fa[pl.ds(row, CHUNKS, stride=8), :] = jnp.zeros((CHUNKS, PATH), f32)

    def spread_y(src, dst):
        return [go(src.at[rows(y_to[d] * 64, 64)], dst.at[d], dev_y[d]) for d in range(3)]

    def spread_z(src, dst):
        return [go(src.at[rows(z_to[d] * 8, 8)], dst.at[d], dev_z[d]) for d in range(7)]

    def send_z(buf):
        piece = buf.at[rows(s * 8, 8)]
        return [go(piece, piece, dev_z[d]) for d in range(7)]

    def send_y(buf):
        band = buf.at[rows(yy * 64, 64)]
        return [go(band, band, dev_y[d]) for d in range(3)]

    def arrive(copies):
        for c in copies:
            c.wait_recv()

    def sum_y(src, got, dst):
        dst[...] = (src[rows(yy * 64, 64), :] + got[0]) + (got[1] + got[2])

    def sum_z(src, got):
        v = [src[rows(zz * 8, 8), :]] + [got[d] for d in range(7)]
        return ((v[0] + v[1]) + (v[2] + v[3])) + ((v[4] + v[5]) + (v[6] + v[7]))

    a1 = spread_y(fa, rya)
    for e in range(8):
        fb[pl.ds(e, CHUNKS, stride=8), :] = acc[pl.ds(ps[3] + 2 * e, CHUNKS, stride=16), :]

    for c in consts[2:]:
        c.wait()
    lane = lax.broadcasted_iota(jnp.int32, (1, PATH), 1)
    rowi = lax.broadcasted_iota(jnp.int32, (NSUB, 1), 0)
    qpad = small_ref[0]
    for l in range(1, LEVELS):
        start = (t // (8 >> l)) * (ROWS * (8 >> l)) + ps[l]
        ca, sa = lane_turn(lane, [start - (t // (8 >> m)) * (ROWS * (8 >> m)) - ps[m] for m in range(LEVELS)])
        table = bcs[l - 1] * ca - bss[l - 1] * sa
        tab[l - 1, 0:NSUB, :] = table
        tab[l - 1, NSUB:, :] = dot32(qpad, table, 0, 0)[:RANK]
    tt[...] = (cs[0] * cv - cs[1] * sv).T

    arrive(a1)
    sum_y(fa, rya, qa)
    a2 = spread_z(qa, rza)
    b1 = spread_y(fb, ryb)
    arrive(a2)
    xb[t] = sum_z(qa, rza)
    a3 = [go(xb.at[t], xb.at[t], dev_t[d]) for d in range(7)]
    arrive(b1)
    sum_y(fb, ryb, qb)
    b2 = spread_z(qb, rzb)
    arrive(a3)
    two = t // 2 * 2
    quad = t // 4 * 4
    for i in range(4):
        cb[2 * i : 2 * i + 2, :] = xb[quad + i][4:6]
    for i in range(8):
        cb[8 + i : 9 + i, :] = xb[i][6:7]
    lane8 = lax.broadcasted_iota(jnp.int32, (8, PATH), 1)
    gc[rows(s * 8, 8), :] = jnp.where(lane8 < 64, cb[0:8, :], pltpu.roll(cb[8:16, :], 64, 1))
    c4 = send_z(gc)
    gb[rows(s * 8, 8), :] = jnp.concatenate([xb[two][0:4], xb[two + 1][0:4]], axis=0)
    b4 = send_z(gb)
    arrive(c4)
    c5 = send_y(gc)
    arrive(b4)
    b5 = send_y(gb)
    arrive(b2)
    gt[rows(s * 8, 8), :] = sum_z(qb, rzb)
    t4 = send_z(gt)

    sub = lax.broadcasted_iota(jnp.int32, (RANK, PATH), 0)
    lan = lax.broadcasted_iota(jnp.int32, (RANK, PATH), 1)
    eye = (sub == lan).astype(f32)
    eye_next = (sub + RANK == lan).astype(f32)
    rblk = lax.broadcasted_iota(jnp.int32, (PATH, PATH), 0) // RANK
    cblk = lax.broadcasted_iota(jnp.int32, (PATH, PATH), 1) // RANK
    wq = small_ref[1]
    head_q = small_ref[2]
    gram, seen, fits = [], [], []

    def take_in(l):
        v = jnp.where(lane < RANK * (l + 1), lv[l], 0.0)
        seen.append(v)
        gram.append(dot32(qpad, v, 0, 0)[:RANK])

    def fill(blocks):
        rest = PATH - RANK * len(blocks)
        return jnp.concatenate(blocks + ([jnp.zeros((rest, PATH), f32)] if rest else []), axis=0)

    def whole_gram():
        low = fill(gram)
        return jnp.where(cblk <= rblk, low, low.T)

    def trace(v):
        return jnp.sum(jnp.sum(v * eye, axis=0, keepdims=True), axis=1, keepdims=True)

    def level_fit(l, part, comb):
        rt = dot3(part, fill([comb]), 1, 1) if l else part
        right = (
            jnp.where(rowi < NSUB - 1, rt, 0.0)
            + pltpu.roll(jnp.where(rowi > 0, pltpu.roll(rt, RANK, 1), 0.0), NSUB - 1, 0)
            + wq
        )
        narrow = rt[:, :RANK]
        w = dot32(narrow, right, 0, 0)
        head = dot32(narrow, head_q, 0, 0)
        wt = dot32(qpad[:, :RANK], rt, 0, 0)
        ridge_one = 0.1 / RANK * trace(w)
        mode = jnp.where(lan < RANK, 0.5 * (pltpu.roll(w, RANK, 1) + wt), 0.0)
        ridge_two = 0.1 / RANK * trace(mode)
        a, b = eliminate(w + ridge_one * eye, mode + ridge_two * eye + eye_next)
        smooth = head + dot3(w, a, 0, 0)[RANK : 2 * RANK]
        mc = dot32(b, comb, 0, 0)[RANK : 2 * RANK]
        moved = jnp.where((lan >= 64) & (lan < 96), smooth, 0.0)
        if l != 2:
            moved = pltpu.roll(moved, (RANK * l - 64) % PATH, 1)
        fits.append(dot3(moved, mc, 0, 0)[RANK * l : RANK * (l + 1)])
        return moved, mc

    def advance(l, moved, mc):
        full = whole_gram()
        both = tab[l - 1]
        lead = dot3(both, moved, 1, 1)
        comb = (sub + RANK * l == lan).astype(f32) - dot3(lead[NSUB:], mc, 1, 0)
        part = seen[l] - dot3(lead[:NSUB], dot3(mc, full, 1, 0), 1, 0)
        if l > 1:
            n = fill(fits[: l - 1])
            comb = comb - dot3(both[NSUB:], n, 1, 0)
            part = part - dot3(both[:NSUB], dot3(n, full, 1, 0), 1, 0)
        return part, comb

    arrive(c5)
    for i in range(8):
        lv[0, 32 * i : 32 * i + 32, :] = pltpu.roll(gc[pl.ds(i, CHUNKS, stride=8), :], 64, 1)
    for i in range(4):
        for e in range(2):
            lv[1, pl.ds(64 * i + e, CHUNKS, stride=2), :] = gc[pl.ds(2 * i + e, CHUNKS, stride=8), :]
    take_in(0)
    take_in(1)
    moved, mc = level_fit(0, seen[0], eye)
    nxt = advance(1, moved, mc)
    arrive(t4)
    t5 = send_y(gt)
    arrive(b5)
    for i in range(2):
        for e in range(4):
            lv[2, pl.ds(128 * i + e, CHUNKS, stride=4), :] = gb[pl.ds(4 * i + e, CHUNKS, stride=8), :]
    take_in(2)
    moved, mc = level_fit(1, *nxt)
    nxt = advance(2, moved, mc)
    moved, mc = level_fit(2, *nxt)
    arrive(t5)
    lv[3] = gt[...]
    take_in(3)
    nxt = advance(3, moved, mc)
    level_fit(3, *nxt)
    eh, el = split(dot3(tt[...], fill(fits), 1, 0))
    e_ref[:, :PATH] = eh
    e_ref[:, PATH:] = el
    for c in live:
        c.wait_send()


N_COPIES = 24 + 5 * 7 + 5 * 3 + 7


def fit(phase, x, cos_t, sin_t, bc, bs, small):
    hbm = pl.BlockSpec(memory_space=pltpu.HBM)
    vm = pl.BlockSpec(memory_space=pltpu.VMEM)
    return pl.pallas_call(
        fit_kernel,
        in_specs=[pl.BlockSpec(memory_space=pltpu.SMEM)] + [hbm] * 6,
        out_specs=(vm, vm, vm),
        out_shape=(
            jax.ShapeDtypeStruct((ROWS, 2 * PATH), bf16),
            jax.ShapeDtypeStruct((PATH, COLS), f32),
            jax.ShapeDtypeStruct((ROWS, COLS), f32),
        ),
        scratch_shapes=[
            pltpu.VMEM((3 * RANK, HALF), f32),
            pltpu.VMEM((3 * RANK, HALF), f32),
            pltpu.VMEM((3 * RANK, HALF), f32),
            pltpu.VMEM((3, RANK, 256), f32),
            pltpu.VMEM((3, RANK, STEP), f32),
            pltpu.VMEM((3, RANK, 256), f32),
            pltpu.VMEM((3, RANK, 256), f32),
            pltpu.VMEM((2, PATH, ROWS), f32),
            pltpu.VMEM((3, NSUB, PATH), f32),
            pltpu.VMEM((3, NSUB, PATH), f32),
            pltpu.VMEM((3, NSUB, PATH), f32),
            pltpu.VMEM((ROWS, PATH), f32),
            pltpu.VMEM((NSUB, PATH), f32),
            pltpu.VMEM((NSUB, PATH), f32),
            pltpu.VMEM((3, 64, PATH), f32),
            pltpu.VMEM((3, 64, PATH), f32),
            pltpu.VMEM((64, PATH), f32),
            pltpu.VMEM((64, PATH), f32),
            pltpu.VMEM((7, 8, PATH), f32),
            pltpu.VMEM((7, 8, PATH), f32),
            pltpu.VMEM((8, 8, PATH), f32),
            pltpu.VMEM((16, PATH), f32),
            pltpu.VMEM((NSUB, PATH), f32),
            pltpu.VMEM((NSUB, PATH), f32),
            pltpu.VMEM((NSUB, PATH), f32),
            pltpu.VMEM((LEVELS, NSUB, PATH), f32),
            pltpu.VMEM((3, NSUB + RANK, PATH), f32),
            pltpu.VMEM((ROWS, PATH), f32),
            pltpu.SemaphoreType.DMA((6,)),
            pltpu.SemaphoreType.DMA((5,)),
            pltpu.SemaphoreType.DMA((N_COPIES,)),
            pltpu.SemaphoreType.DMA((N_COPIES,)),
        ],
        compiler_params=pltpu.CompilerParams(
            collective_id=0, has_side_effects=True, vmem_limit_bytes=FIT_VMEM
        ),
        name="fit",
    )(phase, x, cos_t, sin_t, bc, bs, small)


def subtract_kernel(e_ref, x_ref, y_ref, o_hbm, rest, osem):
    e = e_ref[...]
    copies = []
    for i in range(6):
        sp = pl.ds(i * STEP, STEP)
        yh, yl = split(y_ref[:, sp])
        fitted = dot(e, jnp.concatenate([yh, yh], axis=0), ((1,), (0,)))
        fitted = fitted + dot(e[:, :PATH], yl, ((1,), (0,)))
        rest[:, sp] = x_ref[:, sp] - fitted
        copies.append(pltpu.make_async_copy(rest.at[:, sp], o_hbm.at[:, sp], osem.at[i]))
        copies[i].start()
    for c in copies:
        c.wait()


def subtract(e, x, y):
    vm = pl.BlockSpec(memory_space=pltpu.VMEM)
    return pl.pallas_call(
        subtract_kernel,
        in_specs=[vm] * 3,
        out_specs=pl.BlockSpec(memory_space=pltpu.HBM),
        out_shape=jax.ShapeDtypeStruct((ROWS, COLS), f32),
        scratch_shapes=[pltpu.VMEM((ROWS, COLS), f32), pltpu.SemaphoreType.DMA((6,))],
        compiler_params=pltpu.CompilerParams(vmem_limit_bytes=SUB_VMEM),
        name="subtract",
    )(e, x, y)


def body(snapshots, sample_phase):
    stay = [
        pltpu.with_memory_space_constraint(v, pltpu.HBM)
        for v in [snapshots] + [jnp.asarray(c) for c in make_constants()]
    ]
    e, y, held = fit(pltpu.with_memory_space_constraint(sample_phase, pltpu.HBM), *stay)
    return subtract(e, held, y)


def solution(mesh):
    return jax.shard_map(
        body,
        mesh=mesh,
        in_specs=(P("tm", "space"), P()),
        out_specs=P("tm", "space"),
        check_vma=False,
    )
```
